256 devices in a mesh: tile: 32 (over y, x, core), comp: 8 (over z).
Axes of the slice: x: 4, y: 4, z: 8, core: 2. Of those that a mesh axis runs over, the one named last changes fastest.
Arguments:
- spectrum: bfloat16 [768, 256, 1024], P('comp', 'tile'), may hold values from 0.049804688 to 2
- sea_mask: int32 [256, 1024], P('tile'), may hold values 0 or 1
- depth_class: int32 [256, 1024], P('tile'), may hold values from 0 to 15
- group_speed: float32 [16, 32], replicated, may hold values from 0.2 to 0.45
- wind_speed: float32 [256, 1024], P('tile'), may hold values from 2 to 20
- wind_dir: float32 [256, 1024], P('tile'), may hold values from -3.140625 to 3.140625
- coupling: bfloat16 [768, 768], replicated, may hold values from -0.21875 to 0.21875
Outputs:
- spectrum_next: bfloat16 [768, 256, 1024], P('comp', 'tile')
The draws below stay inside these ranges and needn't reach their ends.
All inputs are finite; a program needn't handle non-finite values. No bound on the sum of `sea_mask` on one device may be relied on, other than what follows from the above.
Results may differ from the reference program's by a relative error of at most 0.002.
The reference program's roundings to bfloat16 on the way count: a program that leaves them out, or rounds other values in their place, can miss the bound.
Values may be sent and summed in bfloat16 or wider, within the bound.
A program may use at most 64 MiB of HBM per device.

```python
import math
import jax
import jax.numpy as jnp
from jax import lax

K = 24
F = 32
DEPTHS = 16
PSTEPS = 4
SRC_STEPS = 4
NY = 1024
COMPONENTS = 768
NX = 256


def with_ends(result, key, low, high):
    longest = result.shape.index(max(result.shape))
    spots = []
    for shift in (0, 1):
        where = [jax.random.randint(jax.random.fold_in(key, axis), (), 0, length) for axis, length in enumerate(result.shape)]
        where[longest] = (where[longest] + shift) % result.shape[longest]
        spots.append(tuple(where))
    return result.at[spots[0]].set(low).at[spots[1]].set(high)


def block_levels(own_key, extent, cuts, low, largest):
    def one(dim, blocks):
        draws = jax.random.uniform(jax.random.fold_in(jax.random.fold_in(own_key, 6), dim), (blocks,), jnp.float32, low / len(cuts), largest / len(cuts))
        return jnp.repeat(jnp.exp(draws), extent[dim] // blocks).reshape((-1,) + (1,) * (len(extent) - dim - 1))

    factor_of = one(*cuts[0])
    for cut in cuts[1:]:
        factor_of = factor_of * one(*cut)
    return factor_of


def centred(rng, extent, scale, most, dtype=jnp.bfloat16):
    entries = scale * jax.random.normal(rng, extent, jnp.float32)
    return jnp.clip(entries, min=-most, max=most).astype(dtype)


def setup_inputs(seed: int = 0) -> dict:
    splits = jax.random.split(jax.random.key(seed), 8)
    spectrum = jnp.clip(jnp.exp(math.log(2.0) - 3.6927934 * jax.random.uniform(splits[0], (COMPONENTS, NX, NY), jnp.float32) ** block_levels(splits[0], (COMPONENTS, NX, NY), ((0, 8), (1, 32)), -0.2, 0.2)), 0.049804688, 2.0).astype(jnp.bfloat16)
    sea_mask = with_ends((jax.random.randint(splits[1], (NX, NY), 0, 10) < 7).astype(jnp.int32), jax.random.fold_in(splits[1], 1), 0, 1)
    depth_class = with_ends(jax.random.randint(splits[2], (NX, NY), 0, DEPTHS), jax.random.fold_in(splits[2], 1), 0, DEPTHS - 1).astype(jnp.int32)
    group_speed = jnp.clip(jnp.exp(jax.random.uniform(splits[3], (DEPTHS, F), jnp.float32, math.log(0.2), math.log(0.45))), 0.2, 0.45)
    wind_speed = jnp.clip(jnp.exp(math.log(20.0) - 2.3025851 * jax.random.uniform(splits[4], (NX, NY), jnp.float32) ** block_levels(splits[4], (NX, NY), ((0, 32),), -0.2, 0.2)), 2.0, 20.0)
    wind_dir = jnp.clip(jax.random.uniform(splits[5], (NX, NY), jnp.float32, -3.140625, 3.140625), -3.140625, 3.140625)
    coupling = centred(splits[6], (COMPONENTS, COMPONENTS), COMPONENTS ** -0.5, 0.21875)
    return dict(spectrum=spectrum, sea_mask=sea_mask, depth_class=depth_class, group_speed=group_speed, wind_speed=wind_speed, wind_dir=wind_dir, coupling=coupling)


def advect(energy, courant_x, courant_y, sea):
    west_side = jnp.roll(energy, 1, axis=1)
    east_side = jnp.roll(energy, -1, axis=1)
    padded = jnp.pad(energy, ((0, 0), (0, 0), (1, 1)))
    south_side = padded[:, :, :-2]
    north_side = padded[:, :, 2:]
    moved = (energy - jnp.maximum(courant_x, 0.0) * (energy - west_side)
             - jnp.minimum(courant_x, 0.0) * (east_side - energy)
             - jnp.maximum(courant_y, 0.0) * (energy - south_side)
             - jnp.minimum(courant_y, 0.0) * (north_side - energy))
    return moved * sea


def sources(spectra, speed, direction, coupling, freq_index, theta):
    state = spectra.astype(jnp.float32)
    weight = (0.1 * jnp.power(1.1, freq_index))[:, None]
    align = jnp.maximum(jnp.cos(theta[:, None] - direction[None, :]), 0.0)
    grow = (0.004 * jnp.power(1.1, freq_index - 16.0))[:, None] * speed[None, :] * align
    freq_rate = ((freq_index + 1.0) / F)[:, None]
    for step in range(SRC_STEPS):
        total = jnp.sum(weight * state, axis=0)
        sat = total / (total + 100.0)
        nonlin = jnp.dot(coupling, state.astype(jnp.bfloat16), preferred_element_type=jnp.float32)
        state = jnp.maximum(state + 0.5 * ((grow - 0.3 * sat[None, :] * freq_rate) * state + 0.25 * nonlin), 0.0)
    return state.astype(jnp.bfloat16)


def reference(spectrum, sea_mask, depth_class, group_speed, wind_speed, wind_dir, coupling):
    sea = sea_mask.astype(jnp.float32)[None]
    theta_dir = jnp.arange(K).astype(jnp.float32) * (2.0 * math.pi / K)
    by_freq = spectrum.reshape(F, K, NX, NY)

    def propagate(args):
        block, freq = args
        speed = group_speed[depth_class, freq]
        courant_x = speed[None] * jnp.cos(theta_dir)[:, None, None]
        courant_y = speed[None] * jnp.sin(theta_dir)[:, None, None]
        energy = block.astype(jnp.float32)
        for step in range(PSTEPS):
            energy = advect(energy, courant_x, courant_y, sea)
        return energy.astype(jnp.bfloat16)

    propagated = lax.map(propagate, (by_freq, jnp.arange(F).astype(jnp.int32)))
    propagated = propagated.reshape(COMPONENTS, NX, NY)
    comp_index = jnp.arange(COMPONENTS).astype(jnp.int32)
    freq_index = (comp_index // K).astype(jnp.float32)
    theta = (comp_index % K).astype(jnp.float32) * (2.0 * math.pi / K)
    rows_first = jnp.moveaxis(propagated, 1, 0)

    def update(args):
        column, speed, direction = args
        return sources(column, speed, direction, coupling, freq_index, theta)

    updated = lax.map(update, (rows_first, wind_speed, wind_dir))
    return jnp.moveaxis(updated, 0, 1)
```

```python
import functools
import math

import jax
import jax.numpy as jnp
import numpy as np
from jax import lax
from jax.experimental import pallas as pl
from jax.experimental.pallas import tpu as pltpu
from jax.sharding import PartitionSpec as P

K = 24
F = 32
DEPTHS = 16
PSTEPS = 4
SRC_STEPS = 4
COLS = 8
LANES = 128
GROUPS = 2
GCOLS = COLS // GROUPS
BF16 = jnp.bfloat16
F32 = jnp.float32


def tables():
    theta = np.arange(K).astype(np.float32) * np.float32(2.0 * math.pi / K)
    j = np.arange(F).astype(np.float64)
    rows = np.zeros((5, F), np.float32)
    rows[0, :K] = np.abs(np.cos(theta))
    rows[1, :K] = np.abs(np.sin(theta))
    rows[2] = 0.1 * 1.1**j
    rows[3] = 0.5 * 0.004 * 1.1 ** (j - 16.0)
    rows[4] = 0.5 * 0.3 * (j + 1.0) / F
    return rows


def step_kernel(
    parts, tiles,
    tab, table, sea_in, depth_in, wind_speed, wind_dir, spectrum, coupling_in, out,
    block, west, east, near_sea, near_depth, speed, sea, natural, sent, points, couple,
    state, nonlin, rounded, winds, back, turned,
    load_sem, couple_sem, mask_send, mask_recv, halo_send, halo_recv,
    out_send, out_recv, back_send, back_recv, own_sem,
):
    me = lax.axis_index("comp")
    tile = lax.axis_index("tile")
    left = lax.rem(tile + tiles - 1, tiles)
    right = lax.rem(tile + 1, tiles)
    comps, columns, rows = block.shape
    freqs = comps // K
    lane_tiles = rows // LANES
    groups = comps // 8
    per = K // 8
    far_first = sorted(range(1, parts), key=lambda d: -min(d, parts - d))

    def chunk_load(f):
        part = pl.ds(f * K, K)
        return pltpu.make_async_copy(spectrum.at[part], block.at[part], load_sem.at[f])

    def couple_load():
        return pltpu.make_async_copy(coupling_in, couple, couple_sem)

    for f in range(freqs):
        chunk_load(f).start()
    couple_load().start()

    barrier = pltpu.get_barrier_semaphore()
    for d in range(1, parts):
        pl.semaphore_signal(barrier, 1, device_id={"comp": lax.rem(me + d, parts)})
    for side in (left, right):
        pl.semaphore_signal(barrier, 1, device_id={"tile": side})
    pl.semaphore_wait(barrier, parts + 1)

    def mask_copy(side, target, array, which):
        return pltpu.make_async_remote_copy(
            (sea_in, depth_in)[array],
            (near_sea, near_depth)[array].at[side],
            mask_send.at[side, array], mask_recv.at[side, array],
            device_id={"tile": target},
        )

    def halo_copies(f):
        quarter = K // 4
        yield pltpu.make_async_remote_copy(
            spectrum.at[pl.ds(f * K, quarter)], west.at[f, pl.ds(0, quarter)],
            halo_send.at[0, f], halo_recv.at[0, f], device_id={"tile": right})
        yield pltpu.make_async_remote_copy(
            spectrum.at[pl.ds(f * K + 3 * quarter, quarter)], west.at[f, pl.ds(quarter, quarter)],
            halo_send.at[1, f], halo_recv.at[1, f], device_id={"tile": right})
        yield pltpu.make_async_remote_copy(
            spectrum.at[pl.ds(f * K + quarter, 2 * quarter)], east.at[f],
            halo_send.at[2, f], halo_recv.at[2, f], device_id={"tile": left})

    masks = [mask_copy(0, right, 0, 0), mask_copy(0, right, 1, 0), mask_copy(1, left, 0, 0), mask_copy(1, left, 1, 0)]
    for copy in masks:
        copy.start()
    for f in range(freqs):
        for copy in halo_copies(f):
            copy.start()

    def find_speed(where, cells, depth):
        def one(t, carry):
            lanes = pl.ds(pl.multiple_of(t * LANES, LANES), LANES)
            wet = cells[:, lanes].astype(F32)
            row = depth[:, lanes]
            sea[where, :, lanes] = wet
            hits = [row == d for d in range(1, DEPTHS)]
            for f in range(freqs):
                j = me * freqs + f
                value = jnp.full((columns, LANES), table[0, j], F32)
                for d in range(1, DEPTHS):
                    value = jnp.where(hits[d - 1], table[d, j], value)
                speed[where, f, :, lanes] = value * wet
            return carry

        lax.fori_loop(0, lane_tiles, one, 0)

    find_speed(0, sea_in, depth_in)
    for copy in masks:
        copy.wait()
    find_speed(1, near_sea.at[0], near_depth.at[0])
    find_speed(2, near_sea.at[1], near_depth.at[1])

    lane = lax.broadcasted_iota(jnp.int32, (columns, rows), 1)
    sub = lax.broadcasted_iota(jnp.int32, (columns, rows), 0)

    def out_copy(f, d):
        target = lax.rem(me + d, parts)
        return pltpu.make_async_remote_copy(
            sent.at[target, 0, :, pl.ds(per * f, per)],
            points.at[0, :, pl.ds(groups * me + per * f, per)],
            out_send.at[0], out_recv.at[0], device_id={"comp": target})

    def out_copy_rest(d):
        target = lax.rem(me + d, parts)
        return pltpu.make_async_remote_copy(
            sent.at[target, 1], points.at[1, :, pl.ds(groups * me, groups)],
            out_send.at[1], out_recv.at[1], device_id={"comp": target})

    def propagate(f, carry):
        chunk_load(f).wait()
        for copy in halo_copies(f):
            copy.wait()
        for quarter in range(4):
            to_east = quarter in (0, 3)
            to_north = quarter in (0, 1)
            halo = west if to_east else east
            place = 1 if to_east else 2
            first = {0: 0, 3: K // 4, 1: 0, 2: K // 4}[quarter]
            x_shift = 1 if to_east else columns - 1
            y_shift = 1 if to_north else rows - 1
            edge = (sub == 0) if to_east else (sub == columns - 1)
            inside = (lane > 0) if to_north else (lane < rows - 1)

            def one(i, carry, quarter=quarter, halo=halo, place=place, first=first, x_shift=x_shift,
                    y_shift=y_shift, edge=edge, inside=inside):
                k = quarter * (K // 4) + i
                along_x, along_y = tab[0, k], tab[1, k]

                def factors(where):
                    cx = speed[where, f] * along_x
                    cy = speed[where, f] * along_y
                    return cx, jnp.where(inside, cy, 0.0), sea[where] - cx - cy

                mine = block[f * K + k].astype(F32)
                theirs = halo[f, first + i].astype(F32)
                cx, cy, keep = factors(0)
                hx, hy, hkeep = factors(place)
                for step in range(PSTEPS):
                    from_halo = pltpu.roll(theirs, x_shift, 0)
                    up_x = jnp.where(edge, from_halo, pltpu.roll(mine, x_shift, 0))
                    mine = keep * mine + cx * up_x + cy * pltpu.roll(mine, y_shift, 1)
                    if step < PSTEPS - 1:
                        theirs = hkeep * theirs + hx * from_halo + hy * pltpu.roll(theirs, y_shift, 1)
                for p in range(lane_tiles):
                    natural[p, pl.ds(pl.multiple_of(k * 8, 8), 8), :] = mine[:, p * LANES:(p + 1) * LANES]
                return carry

            lax.fori_loop(0, K // 4, one, 0)

        def turn(p, carry):
            for c in range(columns):
                for g in range(per):
                    value = natural[p, pl.ds(64 * g + c, 8, stride=8), :]
                    sent[p, c // GCOLS, c % GCOLS, per * f + g] = value.astype(BF16)
            return carry

        lax.fori_loop(0, lane_tiles, turn, 0)
        for d in far_first:
            out_copy(f, d).start()
        return carry

    lax.fori_loop(0, freqs, propagate, 0)
    for d in far_first:
        out_copy_rest(d).start()

    def own_out(g):
        return pltpu.make_async_copy(
            sent.at[me, g], points.at[g, :, pl.ds(groups * me, groups)], own_sem.at[g])

    for g in range(GROUPS):
        own_out(g).start()

    rows_here = pl.ds(pl.multiple_of(me * LANES, LANES), LANES)
    direction = lax.broadcasted_iota(jnp.int32, (K, LANES), 0).astype(F32) * (2.0 * math.pi / K)
    for c in range(columns):
        blow = wind_speed[c:c + 1, rows_here]
        heading = wind_dir[c:c + 1, rows_here]
        align = jnp.maximum(jnp.cos(direction - heading), 0.0)
        winds[c // GCOLS, :, (c % GCOLS) * LANES:(c % GCOLS + 1) * LANES] = blow * align
    couple_load().wait()

    total_comps = parts * comps
    two = 2 * K
    width = GCOLS * LANES

    def own_back(g):
        return pltpu.make_async_copy(
            rounded.at[g, pl.ds(pl.multiple_of(comps * me, comps), comps)], back.at[me, g], own_sem.at[2 + g])

    def source(g, carry):
        pltpu.make_async_copy(
            points.at[g, :, pl.ds(0, groups * (parts - 1))],
            points.at[g, :, pl.ds(0, groups * (parts - 1))], out_recv.at[g]).wait()
        own_out(g).wait()

        def weigh(jj, acc, news):
            for h in range(2):
                folded = news[h][0:8] + news[h][8:16] + news[h][16:24]
                acc = acc + tab[2, 2 * jj + h] * folded
            return acc

        def start(jj, acc):
            at = pl.ds(pl.multiple_of(two * jj, two), two)
            news = []
            for c in range(GCOLS):
                news.append(points[g, c, pl.ds(two // 8 * jj, two // 8)].astype(F32).reshape(two, LANES))
            whole = jnp.concatenate(news, axis=1)
            state[at, :] = whole
            rounded[g, at, :] = whole.astype(BF16)
            return weigh(jj, acc, (whole[:K], whole[K:]))

        zero = jnp.zeros((8, width), F32)
        acc = lax.fori_loop(0, total_comps // two, start, zero)

        def step(s, acc):
            total = jnp.sum(acc, axis=0, keepdims=True)
            sat = jnp.broadcast_to(total / (total + 100.0), (8, width))
            nonlin[...] = jnp.dot(couple[...], rounded[g], preferred_element_type=F32)

            def update(jj, acc):
                news = []
                for h in range(2):
                    at = pl.ds(pl.multiple_of(two * jj + K * h, K), K)
                    j = 2 * jj + h
                    level = 1.0 - tab[4, j] * sat
                    levels = jnp.concatenate([level] * per, axis=0)
                    rate = levels + tab[3, j] * winds[g]
                    new = jnp.maximum(state[at, :] * rate + 0.125 * nonlin[at, :], 0.0)
                    state[at, :] = new
                    news.append(new)
                rounded[g, pl.ds(pl.multiple_of(two * jj, two), two), :] = jnp.concatenate(news, axis=0).astype(BF16)
                return weigh(jj, acc, news)

            return lax.fori_loop(0, total_comps // two, update, zero)

        lax.fori_loop(0, SRC_STEPS, step, acc)
        for d in far_first:
            target = lax.rem(me + d, parts)
            pltpu.make_async_remote_copy(
                rounded.at[g, pl.ds(pl.multiple_of(comps * target, comps), comps)], back.at[me, g],
                back_send.at[g], back_recv.at[g], device_id={"comp": target}).start()
        own_back(g).start()
        return carry

    lax.fori_loop(0, GROUPS, source, 0)

    def settle(g):
        pltpu.make_async_copy(
            back.at[pl.ds(0, parts - 1), g], back.at[pl.ds(0, parts - 1), g], back_recv.at[g]).wait()
        own_back(g).wait()

    settle(0)

    def place(g):
        def one(p, carry):
            for c in range(GCOLS):
                value = back[p, g, :, c * LANES:(c + 1) * LANES].astype(F32)
                turned[p, pl.ds(g * GCOLS + c, comps, stride=8), :] = value
            return carry

        lax.fori_loop(0, lane_tiles, one, 0)

    place(0)
    settle(1)
    place(1)

    def finish(p, carry):
        lanes = pl.ds(pl.multiple_of(p * LANES, LANES), LANES)
        out[:, :, lanes] = turned[p].reshape(comps, columns, LANES).astype(BF16)
        return carry

    lax.fori_loop(0, lane_tiles, finish, 0)

    for g in range(GROUPS):
        pltpu.make_async_copy(
            sent.at[pl.ds(0, parts - 1), g], sent.at[pl.ds(0, parts - 1), g], out_send.at[g]).wait()
        span = pl.ds(0, comps * (parts - 1))
        pltpu.make_async_copy(rounded.at[g, span], rounded.at[g, span], back_send.at[g]).wait()


def on_device(parts, tiles, spectrum, sea_mask, depth_class, group_speed, wind_speed, wind_dir, coupling):
    comps, columns, rows = spectrum.shape
    freqs = comps // K
    whole = comps * parts
    width = GCOLS * LANES
    tab = jnp.asarray(tables())
    vmem, smem, anywhere = (pl.BlockSpec(memory_space=m) for m in (pltpu.VMEM, pltpu.SMEM, pl.ANY))
    dma = pltpu.SemaphoreType.DMA
    return pl.pallas_call(
        functools.partial(step_kernel, parts, tiles),
        out_shape=jax.ShapeDtypeStruct(spectrum.shape, BF16),
        in_specs=[smem, smem, vmem, vmem, vmem, vmem, anywhere, anywhere],
        out_specs=vmem,
        scratch_shapes=[
            pltpu.VMEM((comps, columns, rows), BF16),
            pltpu.VMEM((freqs, K // 2, columns, rows), BF16),
            pltpu.VMEM((freqs, K // 2, columns, rows), BF16),
            pltpu.VMEM((2, columns, rows), jnp.int32),
            pltpu.VMEM((2, columns, rows), jnp.int32),
            pltpu.VMEM((3, freqs, columns, rows), F32),
            pltpu.VMEM((3, columns, rows), F32),
            pltpu.VMEM((parts, K * 8, LANES), F32),
            pltpu.VMEM((parts, GROUPS, GCOLS, comps // 8, 8, LANES), BF16),
            pltpu.VMEM((GROUPS, GCOLS, whole // 8, 8, LANES), BF16),
            pltpu.VMEM((whole, whole), BF16),
            pltpu.VMEM((whole, width), F32),
            pltpu.VMEM((whole, width), F32),
            pltpu.VMEM((GROUPS, whole, width), BF16),
            pltpu.VMEM((GROUPS, K, width), F32),
            pltpu.VMEM((parts, GROUPS, comps, width), BF16),
            pltpu.VMEM((parts, comps * 8, LANES), F32),
            dma((freqs,)), dma,
            dma((2, 2)), dma((2, 2)), dma((3, freqs)), dma((3, freqs)),
            dma((GROUPS,)), dma((GROUPS,)), dma((GROUPS,)), dma((GROUPS,)), dma((2 * GROUPS,)),
        ],
        compiler_params=pltpu.CompilerParams(collective_id=0, has_side_effects=True, vmem_limit_bytes=48 << 20),
    )(tab, group_speed, sea_mask, depth_class, wind_speed, wind_dir, spectrum, coupling)


def solution(mesh):
    placed = (
        P("comp", "tile", None),
        P("tile", None),
        P("tile", None),
        P(),
        P("tile", None),
        P("tile", None),
        P(),
    )
    return jax.shard_map(
        functools.partial(on_device, mesh.shape["comp"], mesh.shape["tile"]),
        mesh=mesh, in_specs=placed, out_specs=P("comp", "tile", None), check_vma=False,
    )
```

```python
import functools
import math

import jax
import jax.numpy as jnp
import numpy as np
from jax import lax
from jax.experimental import pallas as pl
from jax.experimental.pallas import tpu as pltpu
from jax.sharding import PartitionSpec as P

K = 24
F = 32
DEPTHS = 16
PSTEPS = 4
SRC_STEPS = 4
COLS = 8
LANES = 128
GROUPS = 2
GCOLS = COLS // GROUPS
BF16 = jnp.bfloat16
F32 = jnp.float32


def tables():
    theta = np.arange(K).astype(np.float32) * np.float32(2.0 * math.pi / K)
    j = np.arange(F).astype(np.float64)
    rows = np.zeros((5, F), np.float32)
    rows[0, :K] = np.abs(np.cos(theta))
    rows[1, :K] = np.abs(np.sin(theta))
    rows[2] = 0.1 * 1.1**j
    rows[3] = 0.5 * 0.004 * 1.1 ** (j - 16.0)
    rows[4] = 0.5 * 0.3 * (j + 1.0) / F
    return rows


def step_kernel(
    parts, tiles,
    tab_in, table_in, sea_in, depth_in, speed_in, dir_in, spectrum, coupling_in, out,
    tab, table, sea_own, depth_own, wind_speed, wind_dir, block, west, east, near_sea, near_depth, speed, sea, natural, sent, points, couple,
    state, nonlin, rounded, winds, back, turned,
    small_sem, load_sem, couple_sem, mask_send, mask_recv, halo_send, halo_recv,
    out_send, out_recv, back_send, back_recv, own_sem,
):
    me = lax.axis_index("comp")
    tile = lax.axis_index("tile")
    left = lax.rem(tile + tiles - 1, tiles)
    right = lax.rem(tile + 1, tiles)
    comps, columns, rows = block.shape
    freqs = comps // K
    lane_tiles = rows // LANES
    groups = comps // 8
    per = K // 8
    far_first = sorted(range(1, parts), key=lambda d: -min(d, parts - d))

    def chunk_load(f):
        part = pl.ds(f * K, K)
        return pltpu.make_async_copy(spectrum.at[part], block.at[part], load_sem.at[f])

    def couple_load():
        return pltpu.make_async_copy(coupling_in, couple, couple_sem)

    smalls = [
        pltpu.make_async_copy(source, target, small_sem.at[i])
        for i, (source, target) in enumerate((
            (table_in, table), (sea_in, sea_own), (depth_in, depth_own),
            (tab_in, tab), (speed_in, wind_speed), (dir_in, wind_dir)))
    ]
    for copy in smalls[:4]:
        copy.start()
    for f in range(freqs):
        chunk_load(f).start()
    for copy in smalls[4:]:
        copy.start()
    couple_load().start()

    barrier = pltpu.get_barrier_semaphore()
    for d in range(1, parts):
        pl.semaphore_signal(barrier, 1, device_id={"comp": lax.rem(me + d, parts)})
    for side in (left, right):
        pl.semaphore_signal(barrier, 1, device_id={"tile": side})
    for copy in smalls[:4]:
        copy.wait()
    pl.semaphore_wait(barrier, parts + 1)

    def mask_copy(side, target, array, which):
        return pltpu.make_async_remote_copy(
            (sea_in, depth_in)[array],
            (near_sea, near_depth)[array].at[side],
            mask_send.at[side, array], mask_recv.at[side, array],
            device_id={"tile": target},
        )

    def halo_copies(f):
        quarter = K // 4
        yield pltpu.make_async_remote_copy(
            spectrum.at[pl.ds(f * K, quarter)], west.at[f, pl.ds(0, quarter)],
            halo_send.at[0, f], halo_recv.at[0, f], device_id={"tile": right})
        yield pltpu.make_async_remote_copy(
            spectrum.at[pl.ds(f * K + 3 * quarter, quarter)], west.at[f, pl.ds(quarter, quarter)],
            halo_send.at[1, f], halo_recv.at[1, f], device_id={"tile": right})
        for half in range(2):
            yield pltpu.make_async_remote_copy(
                spectrum.at[pl.ds(f * K + (1 + half) * quarter, quarter)],
                east.at[f, pl.ds(half * quarter, quarter)],
                halo_send.at[2 + half, f], halo_recv.at[2 + half, f], device_id={"tile": left})

    masks = [mask_copy(0, right, 0, 0), mask_copy(0, right, 1, 0), mask_copy(1, left, 0, 0), mask_copy(1, left, 1, 0)]
    for copy in masks:
        copy.start()
    for f in range(freqs):
        for copy in halo_copies(f):
            copy.start()

    def find_speed(where, cells, depth):
        def one(t, carry):
            lanes = pl.ds(pl.multiple_of(t * LANES, LANES), LANES)
            wet = cells[:, lanes].astype(F32)
            row = depth[:, lanes]
            sea[where, :, lanes] = wet
            hits = [row == d for d in range(1, DEPTHS)]
            for f in range(freqs):
                j = me * freqs + f
                value = jnp.full((columns, LANES), table[0, j], F32)
                for d in range(1, DEPTHS):
                    value = jnp.where(hits[d - 1], table[d, j], value)
                speed[where, f, :, lanes] = value * wet
            return carry

        lax.fori_loop(0, lane_tiles, one, 0)

    find_speed(0, sea_own, depth_own)
    for copy in masks:
        copy.wait()
    find_speed(1, near_sea.at[0], near_depth.at[0])
    find_speed(2, near_sea.at[1], near_depth.at[1])

    lane = lax.broadcasted_iota(jnp.int32, (columns, rows), 1)
    sub = lax.broadcasted_iota(jnp.int32, (columns, rows), 0)

    def out_copy(f, d):
        target = lax.rem(me + d, parts)
        return pltpu.make_async_remote_copy(
            sent.at[target, 0, :, pl.ds(per * f, per)],
            points.at[0, :, pl.ds(groups * me + per * f, per)],
            out_send.at[0], out_recv.at[0], device_id={"comp": target})

    def out_copy_rest(d):
        target = lax.rem(me + d, parts)
        return pltpu.make_async_remote_copy(
            sent.at[target, 1], points.at[1, :, pl.ds(groups * me, groups)],
            out_send.at[1], out_recv.at[1], device_id={"comp": target})

    def propagate(f, carry):
        chunk_load(f).wait()
        halos = list(halo_copies(f))
        for quarter in range(4):
            halos[(0, 2, 3, 1)[quarter]].wait()
            to_east = quarter in (0, 3)
            to_north = quarter in (0, 1)
            halo = west if to_east else east
            place = 1 if to_east else 2
            first = {0: 0, 3: K // 4, 1: 0, 2: K // 4}[quarter]
            x_shift = 1 if to_east else columns - 1
            y_shift = 1 if to_north else rows - 1
            edge = (sub == 0) if to_east else (sub == columns - 1)
            inside = (lane > 0) if to_north else (lane < rows - 1)

            def one(i, carry, quarter=quarter, halo=halo, place=place, first=first, x_shift=x_shift,
                    y_shift=y_shift, edge=edge, inside=inside):
                k = quarter * (K // 4) + i
                along_x, along_y = tab[0, k], tab[1, k]

                def factors(where):
                    cx = speed[where, f] * along_x
                    cy = speed[where, f] * along_y
                    return cx, jnp.where(inside, cy, 0.0), sea[where] - cx - cy

                mine = block[f * K + k].astype(F32)
                theirs = halo[f, first + i].astype(F32)
                cx, cy, keep = factors(0)
                hx, hy, hkeep = factors(place)
                for step in range(PSTEPS):
                    from_halo = pltpu.roll(theirs, x_shift, 0)
                    up_x = jnp.where(edge, from_halo, pltpu.roll(mine, x_shift, 0))
                    mine = keep * mine + cx * up_x + cy * pltpu.roll(mine, y_shift, 1)
                    if step < PSTEPS - 1:
                        theirs = hkeep * theirs + hx * from_halo + hy * pltpu.roll(theirs, y_shift, 1)
                for p in range(lane_tiles):
                    natural[p, pl.ds(pl.multiple_of(k * 8, 8), 8), :] = mine[:, p * LANES:(p + 1) * LANES]
                return carry

            lax.fori_loop(0, K // 4, one, 0, unroll=3)

        def turn(p, carry):
            for c in range(columns):
                for g in range(per):
                    value = natural[p, pl.ds(64 * g + c, 8, stride=8), :]
                    sent[p, c // GCOLS, c % GCOLS, per * f + g] = value.astype(BF16)
            return carry

        lax.fori_loop(0, lane_tiles, turn, 0)
        for d in far_first:
            out_copy(f, d).start()
        return carry

    lax.fori_loop(0, freqs, propagate, 0)
    for d in far_first:
        out_copy_rest(d).start()

    def own_out(g):
        return pltpu.make_async_copy(
            sent.at[me, g], points.at[g, :, pl.ds(groups * me, groups)], own_sem.at[g])

    for g in range(GROUPS):
        own_out(g).start()

    rows_here = pl.ds(pl.multiple_of(me * LANES, LANES), LANES)
    direction = lax.broadcasted_iota(jnp.int32, (K, LANES), 0).astype(F32) * (2.0 * math.pi / K)
    for copy in smalls[4:]:
        copy.wait()
    for c in range(columns):
        blow = wind_speed[c:c + 1, rows_here]
        heading = wind_dir[c:c + 1, rows_here]
        align = jnp.maximum(jnp.cos(direction - heading), 0.0)
        winds[c // GCOLS, :, (c % GCOLS) * LANES:(c % GCOLS + 1) * LANES] = blow * align
    couple_load().wait()

    total_comps = parts * comps
    two = 2 * K
    width = GCOLS * LANES

    def own_back(g):
        return pltpu.make_async_copy(
            rounded.at[g, pl.ds(pl.multiple_of(comps * me, comps), comps)], back.at[me, g], own_sem.at[2 + g])

    def source(g, carry):
        pltpu.make_async_copy(
            points.at[g, :, pl.ds(0, groups * (parts - 1))],
            points.at[g, :, pl.ds(0, groups * (parts - 1))], out_recv.at[g]).wait()
        own_out(g).wait()

        def weigh(jj, acc, news):
            for h in range(2):
                folded = news[h][0:8] + news[h][8:16] + news[h][16:24]
                acc = acc + tab[2, 2 * jj + h] * folded
            return acc

        def start(jj, acc):
            at = pl.ds(pl.multiple_of(two * jj, two), two)
            news = []
            for c in range(GCOLS):
                news.append(points[g, c, pl.ds(two // 8 * jj, two // 8)].astype(F32).reshape(two, LANES))
            whole = jnp.concatenate(news, axis=1)
            state[at, :] = whole
            rounded[g, at, :] = whole.astype(BF16)
            return weigh(jj, acc, (whole[:K], whole[K:]))

        zero = jnp.zeros((8, width), F32)
        acc = lax.fori_loop(0, total_comps // two, start, zero)

        def step(s, acc):
            total = jnp.sum(acc, axis=0, keepdims=True)
            sat = jnp.broadcast_to(total / (total + 100.0), (8, width))
            nonlin[...] = jnp.dot(couple[...], rounded[g], preferred_element_type=F32)

            def update(jj, acc):
                news = []
                for h in range(2):
                    at = pl.ds(pl.multiple_of(two * jj + K * h, K), K)
                    j = 2 * jj + h
                    level = 1.0 - tab[4, j] * sat
                    levels = jnp.concatenate([level] * per, axis=0)
                    rate = levels + tab[3, j] * winds[g]
                    new = jnp.maximum(state[at, :] * rate + 0.125 * nonlin[at, :], 0.0)
                    state[at, :] = new
                    news.append(new)
                rounded[g, pl.ds(pl.multiple_of(two * jj, two), two), :] = jnp.concatenate(news, axis=0).astype(BF16)
                return weigh(jj, acc, news)

            return lax.fori_loop(0, total_comps // two, update, zero)

        lax.fori_loop(0, SRC_STEPS, step, acc)
        for d in far_first:
            target = lax.rem(me + d, parts)
            pltpu.make_async_remote_copy(
                rounded.at[g, pl.ds(pl.multiple_of(comps * target, comps), comps)], back.at[me, g],
                back_send.at[g], back_recv.at[g], device_id={"comp": target}).start()
        own_back(g).start()
        return carry

    lax.fori_loop(0, GROUPS, source, 0)

    def settle(g):
        pltpu.make_async_copy(
            back.at[pl.ds(0, parts - 1), g], back.at[pl.ds(0, parts - 1), g], back_recv.at[g]).wait()
        own_back(g).wait()

    settle(0)

    def place(g):
        def one(p, carry):
            for c in range(GCOLS):
                value = back[p, g, :, c * LANES:(c + 1) * LANES].astype(F32)
                turned[p, pl.ds(g * GCOLS + c, comps, stride=8), :] = value
            return carry

        lax.fori_loop(0, lane_tiles, one, 0)

    place(0)
    settle(1)
    place(1)

    def finish(p, carry):
        lanes = pl.ds(pl.multiple_of(p * LANES, LANES), LANES)
        out[:, :, lanes] = turned[p].reshape(comps, columns, LANES).astype(BF16)
        return carry

    lax.fori_loop(0, lane_tiles, finish, 0)

    for g in range(GROUPS):
        pltpu.make_async_copy(
            sent.at[pl.ds(0, parts - 1), g], sent.at[pl.ds(0, parts - 1), g], out_send.at[g]).wait()
        span = pl.ds(0, comps * (parts - 1))
        pltpu.make_async_copy(rounded.at[g, span], rounded.at[g, span], back_send.at[g]).wait()


def on_device(parts, tiles, spectrum, sea_mask, depth_class, group_speed, wind_speed, wind_dir, coupling):
    comps, columns, rows = spectrum.shape
    freqs = comps // K
    whole = comps * parts
    width = GCOLS * LANES
    tab = jnp.asarray(tables())
    hbm = pl.BlockSpec(memory_space=pltpu.HBM)
    dma = pltpu.SemaphoreType.DMA
    return pl.pallas_call(
        functools.partial(step_kernel, parts, tiles),
        out_shape=jax.ShapeDtypeStruct(spectrum.shape, BF16),
        in_specs=[hbm] * 8,
        out_specs=pl.BlockSpec(memory_space=pltpu.VMEM),
        scratch_shapes=[
            pltpu.SMEM(tab.shape, F32),
            pltpu.SMEM(group_speed.shape, F32),
            pltpu.VMEM((columns, rows), jnp.int32),
            pltpu.VMEM((columns, rows), jnp.int32),
            pltpu.VMEM((columns, rows), F32),
            pltpu.VMEM((columns, rows), F32),
            pltpu.VMEM((comps, columns, rows), BF16),
            pltpu.VMEM((freqs, K // 2, columns, rows), BF16),
            pltpu.VMEM((freqs, K // 2, columns, rows), BF16),
            pltpu.VMEM((2, columns, rows), jnp.int32),
            pltpu.VMEM((2, columns, rows), jnp.int32),
            pltpu.VMEM((3, freqs, columns, rows), F32),
            pltpu.VMEM((3, columns, rows), F32),
            pltpu.VMEM((parts, K * 8, LANES), F32),
            pltpu.VMEM((parts, GROUPS, GCOLS, comps // 8, 8, LANES), BF16),
            pltpu.VMEM((GROUPS, GCOLS, whole // 8, 8, LANES), BF16),
            pltpu.VMEM((whole, whole), BF16),
            pltpu.VMEM((whole, width), F32),
            pltpu.VMEM((whole, width), F32),
            pltpu.VMEM((GROUPS, whole, width), BF16),
            pltpu.VMEM((GROUPS, K, width), F32),
            pltpu.VMEM((parts, GROUPS, comps, width), BF16),
            pltpu.VMEM((parts, comps * 8, LANES), F32),
            dma((6,)), dma((freqs,)), dma,
            dma((2, 2)), dma((2, 2)), dma((4, freqs)), dma((4, freqs)),
            dma((GROUPS,)), dma((GROUPS,)), dma((GROUPS,)), dma((GROUPS,)), dma((2 * GROUPS,)),
        ],
        compiler_params=pltpu.CompilerParams(collective_id=0, has_side_effects=True, vmem_limit_bytes=48 << 20),
    )(*(pltpu.with_memory_space_constraint(a, pltpu.HBM) for a in (tab, group_speed, sea_mask, depth_class, wind_speed, wind_dir, spectrum, coupling)))


def solution(mesh):
    placed = (
        P("comp", "tile", None),
        P("tile", None),
        P("tile", None),
        P(),
        P("tile", None),
        P("tile", None),
        P(),
    )
    return jax.shard_map(
        functools.partial(on_device, mesh.shape["comp"], mesh.shape["tile"]),
        mesh=mesh, in_specs=placed, out_specs=P("comp", "tile", None), check_vma=False,
    )
```

```python
import functools
import math

import jax
import jax.numpy as jnp
import numpy as np
from jax import lax
from jax.experimental import pallas as pl
from jax.experimental.pallas import tpu as pltpu
from jax.sharding import PartitionSpec as P

K = 24
F = 32
DEPTHS = 16
PSTEPS = 4
SRC_STEPS = 4
COLS = 8
LANES = 128
GROUPS = 2
GCOLS = COLS // GROUPS
BF16 = jnp.bfloat16
F32 = jnp.float32


def tables():
    theta = np.arange(K).astype(np.float32) * np.float32(2.0 * math.pi / K)
    j = np.arange(F).astype(np.float64)
    rows = np.zeros((5, F), np.float32)
    rows[0, :K] = np.abs(np.cos(theta))
    rows[1, :K] = np.abs(np.sin(theta))
    rows[2] = 0.1 * 1.1**j
    rows[3] = 0.5 * 0.004 * 1.1 ** (j - 16.0)
    rows[4] = 0.5 * 0.3 * (j + 1.0) / F
    return rows


def step_kernel(
    parts, tiles,
    tab_in, table_in, sea_in, depth_in, speed_in, dir_in, spectrum, coupling_in, out,
    tab, table, sea_own, depth_own, wind_speed, wind_dir, block, west, east, near_sea, near_depth, speed, sea, natural, sent, points, couple,
    state, nonlin, rounded, winds, back, turned,
    small_sem, load_sem, couple_sem, mask_send, mask_recv, halo_send, halo_recv,
    out_send, out_recv, back_send, back_recv, own_sem,
):
    me = lax.axis_index("comp")
    tile = lax.axis_index("tile")
    left = lax.rem(tile + tiles - 1, tiles)
    right = lax.rem(tile + 1, tiles)
    comps, columns, rows = block.shape
    freqs = comps // K
    lane_tiles = rows // LANES
    groups = comps // 8
    per = K // 8
    near_first = sorted(range(1, parts), key=lambda d: min(d, parts - d))

    def chunk_load(f):
        part = pl.ds(f * K, K)
        return pltpu.make_async_copy(spectrum.at[part], block.at[part], load_sem.at[f])

    def couple_load():
        return pltpu.make_async_copy(coupling_in, couple, couple_sem)

    smalls = [
        pltpu.make_async_copy(source, target, small_sem.at[i])
        for i, (source, target) in enumerate((
            (table_in, table), (sea_in, sea_own), (depth_in, depth_own),
            (tab_in, tab), (speed_in, wind_speed), (dir_in, wind_dir)))
    ]
    for copy in smalls[:4]:
        copy.start()
    for f in range(freqs):
        chunk_load(f).start()
    for copy in smalls[4:]:
        copy.start()
    couple_load().start()

    barrier = pltpu.get_barrier_semaphore()
    for d in range(1, parts):
        pl.semaphore_signal(barrier, 1, device_id={"comp": lax.rem(me + d, parts)})
    for side in (left, right):
        pl.semaphore_signal(barrier, 1, device_id={"tile": side})

    quarter_of = K // 4
    half = columns // 2
    lane = lax.broadcasted_iota(jnp.int32, (columns, rows), 1)
    sub = lax.broadcasted_iota(jnp.int32, (columns, rows), 0)
    sub_one = lax.broadcasted_iota(jnp.int32, (columns, LANES), 0)

    def find_speed(window, low_sea, high_sea, low_depth, high_depth):
        def one(t, carry):
            lanes = pl.ds(pl.multiple_of(t * LANES, LANES), LANES)
            wet, row = low_sea[:, lanes].astype(F32), low_depth[:, lanes].astype(F32)
            if window:
                wet = jnp.where(sub_one < half, wet, high_sea[:, lanes].astype(F32))
                row = jnp.where(sub_one < half, row, high_depth[:, lanes].astype(F32))
            sea[window, :, lanes] = wet
            hits = [row == d for d in range(1, DEPTHS)]
            for f in range(freqs):
                j = me * freqs + f
                value = jnp.full((columns, LANES), table[0, j], F32)
                for d in range(1, DEPTHS):
                    value = jnp.where(hits[d - 1], table[d, j], value)
                speed[window, f, :, lanes] = value * wet
            return carry

        lax.fori_loop(0, lane_tiles, one, 0)

    def run(alone, beside, f, quarter, low, count, unroll):
        to_east = quarter in (0, 3)
        to_north = quarter in (0, 1)
        halo = west if to_east else east
        first = quarter_of if quarter in (2, 3) else 0
        x_shift = 1 if to_east else columns - 1
        y_shift = 1 if to_north else rows - 1
        inside = (lane > 0) if to_north else (lane < rows - 1)
        windows = ([0] if alone else []) + ([1 if to_east else 2] if beside else [])

        def one(i, carry):
            k = quarter * quarter_of + low + i
            mine = block[f * K + k].astype(F32)
            results = []
            for window in windows:
                energy = mine
                if window:
                    theirs = halo[f, first + low + i].astype(F32)
                    pair = (mine, theirs) if to_east else (theirs, mine)
                    energy = jnp.where(sub < half, *pair)
                cx = speed[window, f] * tab[0, k]
                cy = speed[window, f] * tab[1, k]
                keep = sea[window] - cx - cy
                cy = jnp.where(inside, cy, 0.0)
                for step in range(PSTEPS):
                    energy = keep * energy + cx * pltpu.roll(energy, x_shift, 0) + cy * pltpu.roll(energy, y_shift, 1)
                results.append(energy)
            at = pl.ds(pl.multiple_of(k * 8, 8), 8)
            for p in range(lane_tiles):
                pieces = [energy[:, p * LANES:(p + 1) * LANES] for energy in results]
                if beside:
                    other = pieces[0] if alone else natural[f, p, at, :]
                    pair = (pieces[-1], other) if to_east else (other, pieces[-1])
                    pieces = [jnp.where(sub_one < half, *pair)]
                natural[f, p, at, :] = pieces[0]
            return carry

        lax.fori_loop(0, count, one, 0, unroll=unroll)

    def slot(f, g):
        return f if g == 1 else freqs + 2 * f + g // 2

    def turn(f, pieces):
        def one(p, carry):
            for c, g in pieces:
                value = natural[f, p, pl.ds(64 * g + c, 8, stride=8), :]
                sent[p, c // GCOLS, c % GCOLS, slot(f, g)] = value.astype(BF16)
            return carry

        lax.fori_loop(0, lane_tiles, one, 0)

    early = [(c, 1) for c in range(GCOLS)]
    late = [(c, g) for c in range(columns) for g in range(per) if (c, g) not in early]

    def out_copy(g, low, count, d):
        target = lax.rem(me + d, parts)
        return pltpu.make_async_remote_copy(
            sent.at[target, g, :, pl.ds(low, count)], points.at[g, :, pl.ds(groups * me + low, count)],
            out_send.at[g], out_recv.at[g], device_id={"comp": target})

    for copy in smalls[:4]:
        copy.wait()
    find_speed(0, sea_own, None, depth_own, None)

    def start_alone(f, carry):
        chunk_load(f).wait()
        run(True, False, f, 1, 2, 4, 4)
        run(True, False, f, 2, 0, 4, 4)
        turn(f, early)
        return carry

    lax.fori_loop(0, freqs, start_alone, 0)
    pl.semaphore_wait(barrier, parts + 1)

    def mask_copy(side, target, array):
        return pltpu.make_async_remote_copy(
            (sea_in, depth_in)[array],
            (near_sea, near_depth)[array].at[side],
            mask_send.at[side, array], mask_recv.at[side, array],
            device_id={"tile": target},
        )

    def halo_copies(f):
        for part, (first, array, low, target) in enumerate((
                (0, west, 0, right), (1, east, 0, left), (2, east, 1, left), (3, west, 1, right))):
            yield pltpu.make_async_remote_copy(
                spectrum.at[pl.ds(f * K + first * quarter_of, quarter_of)],
                array.at[f, pl.ds(low * quarter_of, quarter_of)],
                halo_send.at[part, f], halo_recv.at[part, f], device_id={"tile": target})

    masks = [mask_copy(side, target, array) for side, target in ((0, right), (1, left)) for array in range(2)]
    for copy in masks:
        copy.start()
    for f in range(freqs):
        for copy in halo_copies(f):
            copy.start()
    for d in near_first:
        out_copy(0, 0, freqs, d).start()

    for copy in masks:
        copy.wait()
    find_speed(1, sea_own, near_sea.at[0], depth_own, near_depth.at[0])
    find_speed(2, near_sea.at[1], sea_own, near_depth.at[1], depth_own)

    def with_halo(f, carry):
        halos = list(halo_copies(f))
        halos[0].wait()
        run(True, True, f, 0, 0, 6, 3)
        halos[1].wait()
        run(True, True, f, 1, 0, 2, 2)
        run(False, True, f, 1, 2, 4, 4)
        halos[2].wait()
        run(False, True, f, 2, 0, 4, 4)
        run(True, True, f, 2, 4, 2, 2)
        halos[3].wait()
        run(True, True, f, 3, 0, 6, 3)
        turn(f, late)
        for d in near_first:
            out_copy(0, freqs + 2 * f, 2, d).start()
        return carry

    lax.fori_loop(0, freqs, with_halo, 0)
    for d in near_first:
        out_copy(1, 0, groups, d).start()

    def own_out(g):
        return pltpu.make_async_copy(
            sent.at[me, g], points.at[g, :, pl.ds(groups * me, groups)], own_sem.at[g])

    for g in range(GROUPS):
        own_out(g).start()

    rows_here = pl.ds(pl.multiple_of(me * LANES, LANES), LANES)
    direction = lax.broadcasted_iota(jnp.int32, (K, LANES), 0).astype(F32) * (2.0 * math.pi / K)
    for copy in smalls[4:]:
        copy.wait()
    for c in range(columns):
        blow = wind_speed[c:c + 1, rows_here]
        heading = wind_dir[c:c + 1, rows_here]
        align = jnp.maximum(jnp.cos(direction - heading), 0.0)
        winds[c // GCOLS, :, (c % GCOLS) * LANES:(c % GCOLS + 1) * LANES] = blow * align
    couple_load().wait()

    total_comps = parts * comps
    two = 2 * K
    width = GCOLS * LANES

    def own_back(g):
        return pltpu.make_async_copy(
            rounded.at[g, pl.ds(pl.multiple_of(comps * me, comps), comps)], back.at[me, g], own_sem.at[2 + g])

    def source(g, carry):
        pltpu.make_async_copy(
            points.at[g, :, pl.ds(0, groups * (parts - 1))],
            points.at[g, :, pl.ds(0, groups * (parts - 1))], out_recv.at[g]).wait()
        own_out(g).wait()

        def weigh(jj, acc, news):
            for h in range(2):
                folded = news[h][0:8] + news[h][8:16] + news[h][16:24]
                acc = acc + tab[2, 2 * jj + h] * folded
            return acc

        def start(z, acc):
            for pair in range(freqs // 2):
                at = pl.ds(pl.multiple_of(comps * z + two * pair, two), two)
                lanes = []
                for c in range(GCOLS):
                    lanes.append(jnp.concatenate([
                        points[g, c, groups * z + slot(2 * pair + h, i)].astype(F32)
                        for h in range(2) for i in range(per)], axis=0))
                whole = jnp.concatenate(lanes, axis=1)
                state[at, :] = whole
                rounded[g, at, :] = whole.astype(BF16)
                acc = weigh(freqs // 2 * z + pair, acc, (whole[:K], whole[K:]))
            return acc

        zero = jnp.zeros((8, width), F32)
        acc = lax.fori_loop(0, parts, start, zero)

        def step(s, acc):
            total = jnp.sum(acc, axis=0, keepdims=True)
            sat = jnp.broadcast_to(total / (total + 100.0), (8, width))
            nonlin[...] = jnp.dot(couple[...], rounded[g], preferred_element_type=F32)

            def update(jj, acc):
                news = []
                for h in range(2):
                    at = pl.ds(pl.multiple_of(two * jj + K * h, K), K)
                    j = 2 * jj + h
                    level = 1.0 - tab[4, j] * sat
                    levels = jnp.concatenate([level] * per, axis=0)
                    rate = levels + tab[3, j] * winds[g]
                    new = jnp.maximum(state[at, :] * rate + 0.125 * nonlin[at, :], 0.0)
                    state[at, :] = new
                    news.append(new)
                rounded[g, pl.ds(pl.multiple_of(two * jj, two), two), :] = jnp.concatenate(news, axis=0).astype(BF16)
                return weigh(jj, acc, news)

            return lax.fori_loop(0, total_comps // two, update, zero)

        lax.fori_loop(0, SRC_STEPS, step, acc)
        for d in near_first:
            target = lax.rem(me + d, parts)
            pltpu.make_async_remote_copy(
                rounded.at[g, pl.ds(pl.multiple_of(comps * target, comps), comps)], back.at[me, g],
                back_send.at[g], back_recv.at[g, g * d], device_id={"comp": target}).start()
        own_back(g).start()
        return carry

    lax.fori_loop(0, GROUPS, source, 0)

    pltpu.make_async_copy(
        back.at[pl.ds(0, parts - 1), 0], back.at[pl.ds(0, parts - 1), 0], back_recv.at[0, 0]).wait()
    own_back(0).wait()

    def place(p, g):
        for c in range(GCOLS):
            value = back[p, g, :, c * LANES:(c + 1) * LANES].astype(F32)
            turned[p, pl.ds(g * GCOLS + c, comps, stride=8), :] = value

    def place_first(p, carry):
        place(p, 0)
        return carry

    lax.fori_loop(0, lane_tiles, place_first, 0)

    def finish(p):
        place(p, 1)
        lanes = pl.ds(pl.multiple_of(p * LANES, LANES), LANES)
        out[:, :, lanes] = turned[p].reshape(comps, columns, LANES).astype(BF16)

    own_back(1).wait()
    finish(me)

    def arrived(i, carry):
        d = (i % 2) * (parts - 1 - i // 2) + (1 - i % 2) * (1 + i // 2)
        pltpu.make_async_copy(back.at[0, 1], back.at[0, 1], back_recv.at[1, d]).wait()
        finish(lax.rem(me + parts - d, parts))
        return carry

    lax.fori_loop(0, parts - 1, arrived, 0)

    for g in range(GROUPS):
        pltpu.make_async_copy(
            sent.at[pl.ds(0, parts - 1), g], sent.at[pl.ds(0, parts - 1), g], out_send.at[g]).wait()
        span = pl.ds(0, comps * (parts - 1))
        pltpu.make_async_copy(rounded.at[g, span], rounded.at[g, span], back_send.at[g]).wait()


def on_device(parts, tiles, spectrum, sea_mask, depth_class, group_speed, wind_speed, wind_dir, coupling):
    comps, columns, rows = spectrum.shape
    freqs = comps // K
    whole = comps * parts
    width = GCOLS * LANES
    tab = jnp.asarray(tables())
    hbm = pl.BlockSpec(memory_space=pltpu.HBM)
    dma = pltpu.SemaphoreType.DMA
    return pl.pallas_call(
        functools.partial(step_kernel, parts, tiles),
        out_shape=jax.ShapeDtypeStruct(spectrum.shape, BF16),
        in_specs=[hbm] * 8,
        out_specs=pl.BlockSpec(memory_space=pltpu.VMEM),
        scratch_shapes=[
            pltpu.SMEM(tab.shape, F32),
            pltpu.SMEM(group_speed.shape, F32),
            pltpu.VMEM((columns, rows), jnp.int32),
            pltpu.VMEM((columns, rows), jnp.int32),
            pltpu.VMEM((columns, rows), F32),
            pltpu.VMEM((columns, rows), F32),
            pltpu.VMEM((comps, columns, rows), BF16),
            pltpu.VMEM((freqs, K // 2, columns, rows), BF16),
            pltpu.VMEM((freqs, K // 2, columns, rows), BF16),
            pltpu.VMEM((2, columns, rows), jnp.int32),
            pltpu.VMEM((2, columns, rows), jnp.int32),
            pltpu.VMEM((3, freqs, columns, rows), F32),
            pltpu.VMEM((3, columns, rows), F32),
            pltpu.VMEM((freqs, parts, K * 8, LANES), F32),
            pltpu.VMEM((parts, GROUPS, GCOLS, comps // 8, 8, LANES), BF16),
            pltpu.VMEM((GROUPS, GCOLS, whole // 8, 8, LANES), BF16),
            pltpu.VMEM((whole, whole), BF16),
            pltpu.VMEM((whole, width), F32),
            pltpu.VMEM((whole, width), F32),
            pltpu.VMEM((GROUPS, whole, width), BF16),
            pltpu.VMEM((GROUPS, K, width), F32),
            pltpu.VMEM((parts, GROUPS, comps, width), BF16),
            pltpu.VMEM((parts, comps * 8, LANES), F32),
            dma((6,)), dma((freqs,)), dma,
            dma((2, 2)), dma((2, 2)), dma((4, freqs)), dma((4, freqs)),
            dma((GROUPS,)), dma((GROUPS,)), dma((GROUPS,)), dma((GROUPS, parts)), dma((2 * GROUPS,)),
        ],
        compiler_params=pltpu.CompilerParams(collective_id=0, has_side_effects=True, vmem_limit_bytes=48 << 20),
    )(*(pltpu.with_memory_space_constraint(a, pltpu.HBM) for a in (tab, group_speed, sea_mask, depth_class, wind_speed, wind_dir, spectrum, coupling)))


def solution(mesh):
    placed = (
        P("comp", "tile", None),
        P("tile", None),
        P("tile", None),
        P(),
        P("tile", None),
        P("tile", None),
        P(),
    )
    return jax.shard_map(
        functools.partial(on_device, mesh.shape["comp"], mesh.shape["tile"]),
        mesh=mesh, in_specs=placed, out_specs=P("comp", "tile", None), check_vma=False,
    )
```

```python
import functools
import math

import jax
import jax.numpy as jnp
import numpy as np
from jax import lax
from jax.experimental import pallas as pl
from jax.experimental.pallas import tpu as pltpu
from jax.sharding import PartitionSpec as P

K = 24
F = 32
DEPTHS = 16
PSTEPS = 4
SRC_STEPS = 4
COLS = 8
LANES = 128
GROUPS = 2
GCOLS = COLS // GROUPS
BF16 = jnp.bfloat16
F32 = jnp.float32


def tables():
    theta = np.arange(K).astype(np.float32) * np.float32(2.0 * math.pi / K)
    j = np.arange(F).astype(np.float64)
    rows = np.zeros((5, F), np.float32)
    rows[0, :K] = np.abs(np.cos(theta))
    rows[1, :K] = np.abs(np.sin(theta))
    rows[2] = 0.1 * 1.1**j
    rows[3] = 0.5 * 0.004 * 1.1 ** (j - 16.0)
    rows[4] = 0.5 * 0.3 * (j + 1.0) / F
    return rows


def step_kernel(
    parts, tiles,
    tab_in, table_in, sea_in, depth_in, speed_in, dir_in, spectrum, coupling_in, out,
    tab, table, sea_own, depth_own, wind_speed, wind_dir, block, west, east, near_sea, near_depth, speed, sea, natural, sent, points, couple,
    state, nonlin, rounded, winds, back, turned,
    small_sem, load_sem, couple_sem, mask_send, mask_recv, halo_send, halo_recv,
    out_send, out_recv, back_send, back_recv, own_sem,
):
    me = lax.axis_index("comp")
    tile = lax.axis_index("tile")
    left = lax.rem(tile + tiles - 1, tiles)
    right = lax.rem(tile + 1, tiles)
    comps, columns, rows = block.shape
    freqs = comps // K
    lane_tiles = rows // LANES
    groups = comps // 8
    per = K // 8
    near_first = sorted(range(1, parts), key=lambda d: min(d, parts - d))

    def chunk_load(f):
        part = pl.ds(f * K, K)
        return pltpu.make_async_copy(spectrum.at[part], block.at[part], load_sem.at[f])

    def couple_load():
        return pltpu.make_async_copy(coupling_in, couple, couple_sem)

    smalls = [
        pltpu.make_async_copy(source, target, small_sem.at[i])
        for i, (source, target) in enumerate((
            (table_in, table), (sea_in, sea_own), (depth_in, depth_own),
            (tab_in, tab), (speed_in, wind_speed), (dir_in, wind_dir)))
    ]
    for copy in smalls[:4]:
        copy.start()
    for f in range(freqs):
        chunk_load(f).start()
    for copy in smalls[4:]:
        copy.start()
    couple_load().start()

    barrier = pltpu.get_barrier_semaphore()
    for d in range(1, parts):
        pl.semaphore_signal(barrier, 1, device_id={"comp": lax.rem(me + d, parts)})
    for side in (left, right):
        pl.semaphore_signal(barrier, 1, device_id={"tile": side})

    quarter_of = K // 4
    half = columns // 2
    lane = lax.broadcasted_iota(jnp.int32, (columns, rows), 1)
    sub = lax.broadcasted_iota(jnp.int32, (columns, rows), 0)
    sub_one = lax.broadcasted_iota(jnp.int32, (columns, LANES), 0)

    def find_speed(window, low_sea, high_sea, low_depth, high_depth):
        wet, row = low_sea[...].astype(F32), low_depth[...].astype(F32)
        if window:
            wet = jnp.where(sub < half, wet, high_sea[...].astype(F32))
            row = jnp.where(sub < half, row, high_depth[...].astype(F32))
        sea[window] = wet

        def one(f, carry):
            j = me * freqs + f
            value = jnp.full((columns, rows), table[0, j], F32)
            for d in range(1, DEPTHS):
                value = jnp.where(row == d, table[d, j], value)
            speed[window, f] = value * wet
            return carry

        lax.fori_loop(0, freqs, one, 0)

    def run(alone, beside, f, quarter, low, count, unroll):
        to_east = quarter in (0, 3)
        to_north = quarter in (0, 1)
        halo = west if to_east else east
        first = quarter_of if quarter in (2, 3) else 0
        x_shift = 1 if to_east else columns - 1
        y_shift = 1 if to_north else rows - 1
        inside = (lane > 0) if to_north else (lane < rows - 1)
        windows = ([0] if alone else []) + ([1 if to_east else 2] if beside else [])

        def one(i, carry):
            k = quarter * quarter_of + low + i
            mine = block[f * K + k].astype(F32)
            results = []
            for window in windows:
                energy = mine
                if window:
                    theirs = halo[f, first + low + i].astype(F32)
                    pair = (mine, theirs) if to_east else (theirs, mine)
                    energy = jnp.where(sub < half, *pair)
                cx = speed[window, f] * tab[0, k]
                cy = speed[window, f] * tab[1, k]
                keep = sea[window] - cx - cy
                cy = jnp.where(inside, cy, 0.0)
                for step in range(PSTEPS):
                    energy = keep * energy + cx * pltpu.roll(energy, x_shift, 0) + cy * pltpu.roll(energy, y_shift, 1)
                results.append(energy)
            at = pl.ds(pl.multiple_of(k * 8, 8), 8)
            for p in range(lane_tiles):
                pieces = [energy[:, p * LANES:(p + 1) * LANES] for energy in results]
                if beside:
                    other = pieces[0] if alone else natural[f, p, at, :]
                    pair = (pieces[-1], other) if to_east else (other, pieces[-1])
                    pieces = [jnp.where(sub_one < half, *pair)]
                natural[f, p, at, :] = pieces[0]
            return carry

        lax.fori_loop(0, count, one, 0, unroll=unroll)

    def slot(f, g):
        return f if g == 1 else freqs + 2 * f + g // 2

    def turn(f, pieces):
        def one(p, carry):
            for c, g in pieces:
                value = natural[f, p, pl.ds(64 * g + c, 8, stride=8), :]
                sent[p, c // GCOLS, c % GCOLS, slot(f, g)] = value.astype(BF16)
            return carry

        lax.fori_loop(0, lane_tiles, one, 0)

    early = [(c, 1) for c in range(GCOLS)]
    late = [(c, g) for c in range(GCOLS, columns) for g in range(per)]

    def out_copy(g, low, count, d):
        target = lax.rem(me + d, parts)
        return pltpu.make_async_remote_copy(
            sent.at[target, g, :, pl.ds(low, count)], points.at[g, :, pl.ds(groups * me + low, count)],
            out_send.at[g], out_recv.at[g], device_id={"comp": target})

    for copy in smalls[:4]:
        copy.wait()
    find_speed(0, sea_own, None, depth_own, None)

    def start_alone(f, carry):
        chunk_load(f).wait()
        run(True, False, f, 1, 2, 4, 4)
        run(True, False, f, 2, 0, 4, 4)
        turn(f, early)
        return carry

    start_alone(0, 0)
    pl.semaphore_wait(barrier, parts + 1)

    def mask_copy(side, target, array):
        return pltpu.make_async_remote_copy(
            (sea_in, depth_in)[array],
            (near_sea, near_depth)[array].at[side],
            mask_send.at[side, array], mask_recv.at[side, array],
            device_id={"tile": target},
        )

    def halo_copies(f):
        for part, (first, array, low, target) in enumerate((
                (0, west, 0, right), (1, east, 0, left), (2, east, 1, left), (3, west, 1, right))):
            yield pltpu.make_async_remote_copy(
                spectrum.at[pl.ds(f * K + first * quarter_of, quarter_of)],
                array.at[f, pl.ds(low * quarter_of, quarter_of)],
                halo_send.at[part, f], halo_recv.at[part, f], device_id={"tile": target})

    masks = [mask_copy(side, target, array) for side, target in ((0, right), (1, left)) for array in range(2)]
    for copy in masks:
        copy.start()
    for f in range(freqs):
        for copy in halo_copies(f):
            copy.start()
    for f in range(freqs):
        if f:
            start_alone(f, 0)
        for d in near_first:
            out_copy(0, f, 1, d).start()

    for copy in masks:
        copy.wait()
    find_speed(1, sea_own, near_sea.at[0], depth_own, near_depth.at[0])
    find_speed(2, near_sea.at[1], sea_own, near_depth.at[1], depth_own)

    def finished(f, g):
        turn(f, [(c, g) for c in range(GCOLS)])
        for d in near_first:
            out_copy(0, slot(f, g), 1, d).start()

    def with_halo(f, carry):
        halos = list(halo_copies(f))
        halos[0].wait()
        run(True, True, f, 0, 0, 6, 3)
        halos[1].wait()
        run(True, True, f, 1, 0, 2, 2)
        finished(f, 0)
        run(False, True, f, 1, 2, 4, 4)
        halos[2].wait()
        run(False, True, f, 2, 0, 4, 4)
        run(True, True, f, 2, 4, 2, 2)
        halos[3].wait()
        run(True, True, f, 3, 0, 6, 3)
        finished(f, 2)
        turn(f, late)
        return carry

    lax.fori_loop(0, freqs, with_halo, 0)
    for d in near_first:
        out_copy(1, 0, groups, d).start()

    def own_out(g):
        return pltpu.make_async_copy(
            sent.at[me, g], points.at[g, :, pl.ds(groups * me, groups)], own_sem.at[g])

    for g in range(GROUPS):
        own_out(g).start()

    rows_here = pl.ds(pl.multiple_of(me * LANES, LANES), LANES)
    direction = lax.broadcasted_iota(jnp.int32, (K, LANES), 0).astype(F32) * (2.0 * math.pi / K)
    for copy in smalls[4:]:
        copy.wait()
    for c in range(columns):
        blow = wind_speed[c:c + 1, rows_here]
        heading = wind_dir[c:c + 1, rows_here]
        align = jnp.maximum(jnp.cos(direction - heading), 0.0)
        winds[c // GCOLS, :, (c % GCOLS) * LANES:(c % GCOLS + 1) * LANES] = blow * align
    couple_load().wait()

    total_comps = parts * comps
    two = 2 * K
    width = GCOLS * LANES

    def own_back(g):
        return pltpu.make_async_copy(
            rounded.at[g, pl.ds(pl.multiple_of(comps * me, comps), comps)], back.at[me, g], own_sem.at[2 + g])

    def source(g, carry):
        pltpu.make_async_copy(
            points.at[g, :, pl.ds(0, groups * (parts - 1))],
            points.at[g, :, pl.ds(0, groups * (parts - 1))], out_recv.at[g]).wait()
        own_out(g).wait()

        def weigh(jj, acc, news):
            for h in range(2):
                folded = news[h][0:8] + news[h][8:16] + news[h][16:24]
                acc = acc + tab[2, 2 * jj + h] * folded
            return acc

        def start(z, acc):
            for pair in range(freqs // 2):
                at = pl.ds(pl.multiple_of(comps * z + two * pair, two), two)
                lanes = []
                for c in range(GCOLS):
                    lanes.append(jnp.concatenate([
                        points[g, c, groups * z + slot(2 * pair + h, i)].astype(F32)
                        for h in range(2) for i in range(per)], axis=0))
                whole = jnp.concatenate(lanes, axis=1)
                state[at, :] = whole
                rounded[g, at, :] = whole.astype(BF16)
                acc = weigh(freqs // 2 * z + pair, acc, (whole[:K], whole[K:]))
            return acc

        zero = jnp.zeros((8, width), F32)
        acc = lax.fori_loop(0, parts, start, zero)

        def step(s, acc):
            total = jnp.sum(acc, axis=0, keepdims=True)
            sat = jnp.broadcast_to(total / (total + 100.0), (8, width))
            nonlin[...] = jnp.dot(couple[...], rounded[g], preferred_element_type=F32)

            def update(jj, acc):
                news = []
                for h in range(2):
                    at = pl.ds(pl.multiple_of(two * jj + K * h, K), K)
                    j = 2 * jj + h
                    level = 1.0 - tab[4, j] * sat
                    levels = jnp.concatenate([level] * per, axis=0)
                    rate = levels + tab[3, j] * winds[g]
                    new = jnp.maximum(state[at, :] * rate + 0.125 * nonlin[at, :], 0.0)
                    state[at, :] = new
                    news.append(new)
                rounded[g, pl.ds(pl.multiple_of(two * jj, two), two), :] = jnp.concatenate(news, axis=0).astype(BF16)
                return weigh(jj, acc, news)

            return lax.fori_loop(0, total_comps // two, update, zero)

        lax.fori_loop(0, SRC_STEPS, step, acc)
        for d in near_first:
            target = lax.rem(me + d, parts)
            pltpu.make_async_remote_copy(
                rounded.at[g, pl.ds(pl.multiple_of(comps * target, comps), comps)], back.at[me, g],
                back_send.at[g], back_recv.at[g, g * d], device_id={"comp": target}).start()
        own_back(g).start()
        return carry

    lax.fori_loop(0, GROUPS, source, 0)

    pltpu.make_async_copy(
        back.at[pl.ds(0, parts - 1), 0], back.at[pl.ds(0, parts - 1), 0], back_recv.at[0, 0]).wait()
    own_back(0).wait()

    def place(p, g):
        for c in range(GCOLS):
            value = back[p, g, :, c * LANES:(c + 1) * LANES].astype(F32)
            turned[p, pl.ds(g * GCOLS + c, comps, stride=8), :] = value

    def place_first(p, carry):
        place(p, 0)
        return carry

    lax.fori_loop(0, lane_tiles, place_first, 0)

    def finish(p):
        place(p, 1)
        lanes = pl.ds(pl.multiple_of(p * LANES, LANES), LANES)
        out[:, :, lanes] = turned[p].reshape(comps, columns, LANES).astype(BF16)

    own_back(1).wait()
    finish(me)

    def arrived(i, carry):
        d = (i % 2) * (parts - 1 - i // 2) + (1 - i % 2) * (1 + i // 2)
        pltpu.make_async_copy(back.at[0, 1], back.at[0, 1], back_recv.at[1, d]).wait()
        finish(lax.rem(me + parts - d, parts))
        return carry

    lax.fori_loop(0, parts - 1, arrived, 0)

    for g in range(GROUPS):
        pltpu.make_async_copy(
            sent.at[pl.ds(0, parts - 1), g], sent.at[pl.ds(0, parts - 1), g], out_send.at[g]).wait()
        span = pl.ds(0, comps * (parts - 1))
        pltpu.make_async_copy(rounded.at[g, span], rounded.at[g, span], back_send.at[g]).wait()


def on_device(parts, tiles, spectrum, sea_mask, depth_class, group_speed, wind_speed, wind_dir, coupling):
    comps, columns, rows = spectrum.shape
    freqs = comps // K
    whole = comps * parts
    width = GCOLS * LANES
    tab = jnp.asarray(tables())
    hbm = pl.BlockSpec(memory_space=pltpu.HBM)
    dma = pltpu.SemaphoreType.DMA
    return pl.pallas_call(
        functools.partial(step_kernel, parts, tiles),
        out_shape=jax.ShapeDtypeStruct(spectrum.shape, BF16),
        in_specs=[hbm] * 8,
        out_specs=pl.BlockSpec(memory_space=pltpu.VMEM),
        scratch_shapes=[
            pltpu.SMEM(tab.shape, F32),
            pltpu.SMEM(group_speed.shape, F32),
            pltpu.VMEM((columns, rows), jnp.int32),
            pltpu.VMEM((columns, rows), jnp.int32),
            pltpu.VMEM((columns, rows), F32),
            pltpu.VMEM((columns, rows), F32),
            pltpu.VMEM((comps, columns, rows), BF16),
            pltpu.VMEM((freqs, K // 2, columns, rows), BF16),
            pltpu.VMEM((freqs, K // 2, columns, rows), BF16),
            pltpu.VMEM((2, columns, rows), jnp.int32),
            pltpu.VMEM((2, columns, rows), jnp.int32),
            pltpu.VMEM((3, freqs, columns, rows), F32),
            pltpu.VMEM((3, columns, rows), F32),
            pltpu.VMEM((freqs, parts, K * 8, LANES), F32),
            pltpu.VMEM((parts, GROUPS, GCOLS, comps // 8, 8, LANES), BF16),
            pltpu.VMEM((GROUPS, GCOLS, whole // 8, 8, LANES), BF16),
            pltpu.VMEM((whole, whole), BF16),
            pltpu.VMEM((whole, width), F32),
            pltpu.VMEM((whole, width), F32),
            pltpu.VMEM((GROUPS, whole, width), BF16),
            pltpu.VMEM((GROUPS, K, width), F32),
            pltpu.VMEM((parts, GROUPS, comps, width), BF16),
            pltpu.VMEM((parts, comps * 8, LANES), F32),
            dma((6,)), dma((freqs,)), dma,
            dma((2, 2)), dma((2, 2)), dma((4, freqs)), dma((4, freqs)),
            dma((GROUPS,)), dma((GROUPS,)), dma((GROUPS,)), dma((GROUPS, parts)), dma((2 * GROUPS,)),
        ],
        compiler_params=pltpu.CompilerParams(collective_id=0, has_side_effects=True, vmem_limit_bytes=48 << 20),
    )(*(pltpu.with_memory_space_constraint(a, pltpu.HBM) for a in (tab, group_speed, sea_mask, depth_class, wind_speed, wind_dir, spectrum, coupling)))


def solution(mesh):
    placed = (
        P("comp", "tile", None),
        P("tile", None),
        P("tile", None),
        P(),
        P("tile", None),
        P("tile", None),
        P(),
    )
    return jax.shard_map(
        functools.partial(on_device, mesh.shape["comp"], mesh.shape["tile"]),
        mesh=mesh, in_specs=placed, out_specs=P("comp", "tile", None), check_vma=False,
    )
```

```python
import functools
import math

import jax
import jax.numpy as jnp
import numpy as np
from jax import lax
from jax.experimental import pallas as pl
from jax.experimental.pallas import tpu as pltpu
from jax.sharding import PartitionSpec as P

K = 24
F = 32
DEPTHS = 16
PSTEPS = 4
SRC_STEPS = 4
COLS = 8
LANES = 128
GROUPS = 2
GCOLS = COLS // GROUPS
AHEAD = 1
BF16 = jnp.bfloat16
F32 = jnp.float32


def tables():
    theta = np.arange(K).astype(np.float32) * np.float32(2.0 * math.pi / K)
    j = np.arange(F).astype(np.float64)
    rows = np.zeros((5, F), np.float32)
    rows[0, :K] = np.abs(np.cos(theta))
    rows[1, :K] = np.abs(np.sin(theta))
    rows[2] = 0.1 * 1.1**j
    rows[3] = 0.5 * 0.004 * 1.1 ** (j - 16.0)
    rows[4] = 0.5 * 0.3 * (j + 1.0) / F
    return rows


def step_kernel(
    parts, tiles,
    tab_in, table_in, sea_in, depth_in, speed_in, dir_in, spectrum, coupling_in, out,
    tab, table, sea_own, depth_own, wind_speed, wind_dir, block, west, east, near_sea, near_depth, speed, sea, natural, sent, points, couple,
    state, nonlin, rounded, winds, back, turned,
    small_sem, load_sem, couple_sem, mask_send, mask_recv, halo_send, halo_recv,
    out_send, out_recv, back_send, back_recv, own_sem,
):
    me = lax.axis_index("comp")
    tile = lax.axis_index("tile")
    left = lax.rem(tile + tiles - 1, tiles)
    right = lax.rem(tile + 1, tiles)
    comps, columns, rows = block.shape
    freqs = comps // K
    lane_tiles = rows // LANES
    groups = comps // 8
    per = K // 8
    near_first = sorted(range(1, parts), key=lambda d: min(d, parts - d))

    def chunk_load(f):
        part = pl.ds(f * K, K)
        return pltpu.make_async_copy(spectrum.at[part], block.at[part], load_sem.at[f])

    def couple_load():
        return pltpu.make_async_copy(coupling_in, couple, couple_sem)

    smalls = [
        pltpu.make_async_copy(source, target, small_sem.at[i])
        for i, (source, target) in enumerate((
            (table_in, table), (sea_in, sea_own), (depth_in, depth_own),
            (tab_in, tab), (speed_in, wind_speed), (dir_in, wind_dir)))
    ]
    for copy in smalls[:4]:
        copy.start()
    for f in range(freqs):
        chunk_load(f).start()
    for copy in smalls[4:]:
        copy.start()
    couple_load().start()

    barrier = pltpu.get_barrier_semaphore()
    for d in range(1, parts):
        pl.semaphore_signal(barrier, 1, device_id={"comp": lax.rem(me + d, parts)})
    for side in (left, right):
        pl.semaphore_signal(barrier, 1, device_id={"tile": side})

    quarter_of = K // 4
    half = columns // 2
    lane = lax.broadcasted_iota(jnp.int32, (columns, rows), 1)
    sub = lax.broadcasted_iota(jnp.int32, (columns, rows), 0)
    sub_one = lax.broadcasted_iota(jnp.int32, (columns, LANES), 0)

    def find_speed(window, low_sea, high_sea, low_depth, high_depth):
        wet, row = low_sea[...].astype(F32), low_depth[...].astype(F32)
        if window:
            wet = jnp.where(sub < half, wet, high_sea[...].astype(F32))
            row = jnp.where(sub < half, row, high_depth[...].astype(F32))
        sea[window] = wet

        def one(f, carry):
            j = me * freqs + f
            value = jnp.full((columns, rows), table[0, j], F32)
            for d in range(1, DEPTHS):
                value = jnp.where(row == d, table[d, j], value)
            speed[window, f] = value * wet
            return carry

        lax.fori_loop(0, freqs, one, 0)

    def run(alone, beside, f, quarter, low, count, unroll):
        to_east = quarter in (0, 3)
        to_north = quarter in (0, 1)
        halo = west if to_east else east
        first = quarter_of if quarter in (2, 3) else 0
        x_shift = 1 if to_east else columns - 1
        y_shift = 1 if to_north else rows - 1
        inside = (lane > 0) if to_north else (lane < rows - 1)
        windows = ([0] if alone else []) + ([1 if to_east else 2] if beside else [])

        def one(i, carry):
            k = quarter * quarter_of + low + i
            mine = block[f * K + k].astype(F32)
            results = []
            for window in windows:
                energy = mine
                if window:
                    theirs = halo[f, first + low + i].astype(F32)
                    pair = (mine, theirs) if to_east else (theirs, mine)
                    energy = jnp.where(sub < half, *pair)
                cx = speed[window, f] * tab[0, k]
                cy = speed[window, f] * tab[1, k]
                keep = sea[window] - cx - cy
                cy = jnp.where(inside, cy, 0.0)
                for step in range(PSTEPS):
                    energy = keep * energy + cx * pltpu.roll(energy, x_shift, 0) + cy * pltpu.roll(energy, y_shift, 1)
                results.append(energy)
            at = pl.ds(pl.multiple_of(k * 8, 8), 8)
            for p in range(lane_tiles):
                pieces = [energy[:, p * LANES:(p + 1) * LANES] for energy in results]
                if beside:
                    other = pieces[0] if alone else natural[f, p, at, :]
                    pair = (pieces[-1], other) if to_east else (other, pieces[-1])
                    pieces = [jnp.where(sub_one < half, *pair)]
                natural[f, p, at, :] = pieces[0]
            return carry

        lax.fori_loop(0, count, one, 0, unroll=unroll)

    def slot(f, g):
        return f if g == 1 else freqs + 2 * f + g // 2

    def turn(f, pieces):
        def one(p, carry):
            for c, g in pieces:
                value = natural[f, p, pl.ds(64 * g + c, 8, stride=8), :]
                sent[p, c // GCOLS, c % GCOLS, slot(f, g)] = value.astype(BF16)
            return carry

        lax.fori_loop(0, lane_tiles, one, 0)

    early = [(c, 1) for c in range(GCOLS)]
    late = [(c, g) for c in range(GCOLS, columns) for g in range(per)]

    def out_copy(g, low, count, d):
        target = lax.rem(me + d, parts)
        return pltpu.make_async_remote_copy(
            sent.at[target, g, :, pl.ds(low, count)], points.at[g, :, pl.ds(groups * me + low, count)],
            out_send.at[g], out_recv.at[g], device_id={"comp": target})

    for copy in smalls[:4]:
        copy.wait()
    find_speed(0, sea_own, None, depth_own, None)

    def start_alone(f, carry):
        chunk_load(f).wait()
        run(True, False, f, 1, 2, 4, 4)
        run(True, False, f, 2, 0, 4, 4)
        turn(f, early)
        return carry

    start_alone(0, 0)
    pl.semaphore_wait(barrier, parts + 1)

    def mask_copy(side, target, array):
        return pltpu.make_async_remote_copy(
            (sea_in, depth_in)[array],
            (near_sea, near_depth)[array].at[side],
            mask_send.at[side, array], mask_recv.at[side, array],
            device_id={"tile": target},
        )

    def halo_copies(f):
        for part, (first, array, low, target) in enumerate((
                (0, west, 0, right), (1, east, 0, left), (2, east, 1, left), (3, west, 1, right))):
            yield pltpu.make_async_remote_copy(
                spectrum.at[pl.ds(f * K + first * quarter_of, quarter_of)],
                array.at[f, pl.ds(low * quarter_of, quarter_of)],
                halo_send.at[part, f], halo_recv.at[part, f], device_id={"tile": target})

    masks = [mask_copy(side, target, array) for side, target in ((0, right), (1, left)) for array in range(2)]
    for copy in masks:
        copy.start()
    for f in range(freqs):
        for copy in halo_copies(f):
            copy.start()
    for f in range(freqs):
        if f:
            start_alone(f, 0)
        for d in near_first:
            out_copy(0, f, 1, d).start()

    for copy in masks:
        copy.wait()
    find_speed(1, sea_own, near_sea.at[0], depth_own, near_depth.at[0])
    find_speed(2, near_sea.at[1], sea_own, near_depth.at[1], depth_own)

    def finished(f, g):
        turn(f, [(c, g) for c in range(GCOLS)])
        for d in near_first:
            out_copy(0, slot(f, g), 1, d).start()

    def with_halo(f, carry):
        halos = list(halo_copies(f))
        halos[0].wait()
        run(True, True, f, 0, 0, 6, 3)
        halos[1].wait()
        run(True, True, f, 1, 0, 2, 2)
        finished(f, 0)
        run(False, True, f, 1, 2, 4, 4)
        halos[2].wait()
        run(False, True, f, 2, 0, 4, 4)
        run(True, True, f, 2, 4, 2, 2)
        halos[3].wait()
        run(True, True, f, 3, 0, 6, 3)
        finished(f, 2)
        turn(f, late)

        @pl.when(f < AHEAD)
        def _():
            for d in near_first:
                out_copy(1, f, 1, d).start()
            for d in near_first:
                out_copy(1, freqs + 2 * f, 2, d).start()

        return carry

    lax.fori_loop(0, freqs, with_halo, 0)
    for d in near_first:
        out_copy(1, AHEAD, freqs - AHEAD, d).start()
    for d in near_first:
        out_copy(1, freqs + 2 * AHEAD, 2 * (freqs - AHEAD), d).start()

    def own_out(g):
        return pltpu.make_async_copy(
            sent.at[me, g], points.at[g, :, pl.ds(groups * me, groups)], own_sem.at[g])

    for g in range(GROUPS):
        own_out(g).start()

    rows_here = pl.ds(pl.multiple_of(me * LANES, LANES), LANES)
    direction = lax.broadcasted_iota(jnp.int32, (K, LANES), 0).astype(F32) * (2.0 * math.pi / K)
    for copy in smalls[4:]:
        copy.wait()
    for c in range(columns):
        blow = wind_speed[c:c + 1, rows_here]
        heading = wind_dir[c:c + 1, rows_here]
        align = jnp.maximum(jnp.cos(direction - heading), 0.0)
        winds[c // GCOLS, :, (c % GCOLS) * LANES:(c % GCOLS + 1) * LANES] = blow * align
    couple_load().wait()

    total_comps = parts * comps
    two = 2 * K
    width = GCOLS * LANES

    def own_back(g):
        return pltpu.make_async_copy(
            rounded.at[g, pl.ds(pl.multiple_of(comps * me, comps), comps)], back.at[me, g], own_sem.at[2 + g])

    def source(g, carry):
        pltpu.make_async_copy(
            points.at[g, :, pl.ds(0, groups * (parts - 1))],
            points.at[g, :, pl.ds(0, groups * (parts - 1))], out_recv.at[g]).wait()
        own_out(g).wait()

        def weigh(jj, acc, news):
            for h in range(2):
                folded = news[h][0:8] + news[h][8:16] + news[h][16:24]
                acc = acc + tab[2, 2 * jj + h] * folded
            return acc

        def start(z, acc):
            for pair in range(freqs // 2):
                at = pl.ds(pl.multiple_of(comps * z + two * pair, two), two)
                lanes = []
                for c in range(GCOLS):
                    lanes.append(jnp.concatenate([
                        points[g, c, groups * z + slot(2 * pair + h, i)].astype(F32)
                        for h in range(2) for i in range(per)], axis=0))
                whole = jnp.concatenate(lanes, axis=1)
                state[at, :] = whole
                rounded[g, at, :] = whole.astype(BF16)
                acc = weigh(freqs // 2 * z + pair, acc, (whole[:K], whole[K:]))
            return acc

        zero = jnp.zeros((8, width), F32)
        acc = lax.fori_loop(0, parts, start, zero)

        def step(s, acc):
            total = jnp.sum(acc, axis=0, keepdims=True)
            sat = jnp.broadcast_to(total / (total + 100.0), (8, width))
            nonlin[...] = jnp.dot(couple[...], rounded[g], preferred_element_type=F32)

            def update(jj, acc):
                news = []
                for h in range(2):
                    at = pl.ds(pl.multiple_of(two * jj + K * h, K), K)
                    j = 2 * jj + h
                    level = 1.0 - tab[4, j] * sat
                    levels = jnp.concatenate([level] * per, axis=0)
                    rate = levels + tab[3, j] * winds[g]
                    new = jnp.maximum(state[at, :] * rate + 0.125 * nonlin[at, :], 0.0)
                    state[at, :] = new
                    news.append(new)
                rounded[g, pl.ds(pl.multiple_of(two * jj, two), two), :] = jnp.concatenate(news, axis=0).astype(BF16)
                return weigh(jj, acc, news)

            return lax.fori_loop(0, total_comps // two, update, zero)

        lax.fori_loop(0, SRC_STEPS, step, acc)
        for d in near_first:
            target = lax.rem(me + d, parts)
            pltpu.make_async_remote_copy(
                rounded.at[g, pl.ds(pl.multiple_of(comps * target, comps), comps)], back.at[me, g],
                back_send.at[g], back_recv.at[g, g * d], device_id={"comp": target}).start()
        own_back(g).start()
        return carry

    lax.fori_loop(0, GROUPS, source, 0)

    pltpu.make_async_copy(
        back.at[pl.ds(0, parts - 1), 0], back.at[pl.ds(0, parts - 1), 0], back_recv.at[0, 0]).wait()
    own_back(0).wait()

    def place(p, g):
        for c in range(GCOLS):
            value = back[p, g, :, c * LANES:(c + 1) * LANES].astype(F32)
            turned[p, pl.ds(g * GCOLS + c, comps, stride=8), :] = value

    def place_first(p, carry):
        place(p, 0)
        return carry

    lax.fori_loop(0, lane_tiles, place_first, 0)

    def finish(p):
        place(p, 1)
        lanes = pl.ds(pl.multiple_of(p * LANES, LANES), LANES)
        out[:, :, lanes] = turned[p].reshape(comps, columns, LANES).astype(BF16)

    own_back(1).wait()
    finish(me)

    def arrived(i, carry):
        d = (i % 2) * (parts - 1 - i // 2) + (1 - i % 2) * (1 + i // 2)
        pltpu.make_async_copy(back.at[0, 1], back.at[0, 1], back_recv.at[1, d]).wait()
        finish(lax.rem(me + parts - d, parts))
        return carry

    lax.fori_loop(0, parts - 1, arrived, 0)

    for g in range(GROUPS):
        pltpu.make_async_copy(
            sent.at[pl.ds(0, parts - 1), g], sent.at[pl.ds(0, parts - 1), g], out_send.at[g]).wait()
        span = pl.ds(0, comps * (parts - 1))
        pltpu.make_async_copy(rounded.at[g, span], rounded.at[g, span], back_send.at[g]).wait()


def on_device(parts, tiles, spectrum, sea_mask, depth_class, group_speed, wind_speed, wind_dir, coupling):
    comps, columns, rows = spectrum.shape
    freqs = comps // K
    whole = comps * parts
    width = GCOLS * LANES
    tab = jnp.asarray(tables())
    hbm = pl.BlockSpec(memory_space=pltpu.HBM)
    dma = pltpu.SemaphoreType.DMA
    return pl.pallas_call(
        functools.partial(step_kernel, parts, tiles),
        out_shape=jax.ShapeDtypeStruct(spectrum.shape, BF16),
        in_specs=[hbm] * 8,
        out_specs=pl.BlockSpec(memory_space=pltpu.VMEM),
        scratch_shapes=[
            pltpu.SMEM(tab.shape, F32),
            pltpu.SMEM(group_speed.shape, F32),
            pltpu.VMEM((columns, rows), jnp.int32),
            pltpu.VMEM((columns, rows), jnp.int32),
            pltpu.VMEM((columns, rows), F32),
            pltpu.VMEM((columns, rows), F32),
            pltpu.VMEM((comps, columns, rows), BF16),
            pltpu.VMEM((freqs, K // 2, columns, rows), BF16),
            pltpu.VMEM((freqs, K // 2, columns, rows), BF16),
            pltpu.VMEM((2, columns, rows), jnp.int32),
            pltpu.VMEM((2, columns, rows), jnp.int32),
            pltpu.VMEM((3, freqs, columns, rows), F32),
            pltpu.VMEM((3, columns, rows), F32),
            pltpu.VMEM((freqs, parts, K * 8, LANES), F32),
            pltpu.VMEM((parts, GROUPS, GCOLS, comps // 8, 8, LANES), BF16),
            pltpu.VMEM((GROUPS, GCOLS, whole // 8, 8, LANES), BF16),
            pltpu.VMEM((whole, whole), BF16),
            pltpu.VMEM((whole, width), F32),
            pltpu.VMEM((whole, width), F32),
            pltpu.VMEM((GROUPS, whole, width), BF16),
            pltpu.VMEM((GROUPS, K, width), F32),
            pltpu.VMEM((parts, GROUPS, comps, width), BF16),
            pltpu.VMEM((parts, comps * 8, LANES), F32),
            dma((6,)), dma((freqs,)), dma,
            dma((2, 2)), dma((2, 2)), dma((4, freqs)), dma((4, freqs)),
            dma((GROUPS,)), dma((GROUPS,)), dma((GROUPS,)), dma((GROUPS, parts)), dma((2 * GROUPS,)),
        ],
        compiler_params=pltpu.CompilerParams(collective_id=0, has_side_effects=True, vmem_limit_bytes=48 << 20),
    )(*(pltpu.with_memory_space_constraint(a, pltpu.HBM) for a in (tab, group_speed, sea_mask, depth_class, wind_speed, wind_dir, spectrum, coupling)))


def solution(mesh):
    placed = (
        P("comp", "tile", None),
        P("tile", None),
        P("tile", None),
        P(),
        P("tile", None),
        P("tile", None),
        P(),
    )
    return jax.shard_map(
        functools.partial(on_device, mesh.shape["comp"], mesh.shape["tile"]),
        mesh=mesh, in_specs=placed, out_specs=P("comp", "tile", None), check_vma=False,
    )
```

```python
import functools
import math

import jax
import jax.numpy as jnp
import numpy as np
from jax import lax
from jax.experimental import pallas as pl
from jax.experimental.pallas import tpu as pltpu
from jax.sharding import PartitionSpec as P

K = 24
F = 32
DEPTHS = 16
PSTEPS = 4
SRC_STEPS = 4
COLS = 8
LANES = 128
GROUPS = 2
GCOLS = COLS // GROUPS
AHEAD = 1
BF16 = jnp.bfloat16
F32 = jnp.float32


def tables():
    theta = np.arange(K).astype(np.float32) * np.float32(2.0 * math.pi / K)
    j = np.arange(F).astype(np.float64)
    rows = np.zeros((5, F), np.float32)
    rows[0, :K] = np.abs(np.cos(theta))
    rows[1, :K] = np.abs(np.sin(theta))
    rows[2] = 0.1 * 1.1**j
    rows[3] = 0.5 * 0.004 * 1.1 ** (j - 16.0)
    rows[4] = 0.5 * 0.3 * (j + 1.0) / F
    return rows


def step_kernel(
    parts, tiles,
    tab_in, table_in, sea_in, depth_in, speed_in, dir_in, spectrum, coupling_in, out,
    tab, table, sea_own, depth_own, wind_speed, wind_dir, block, west, east, near_sea, near_depth, speed, sea, natural, sent, points, couple,
    state, nonlin, rounded, winds, back, turned,
    small_sem, load_sem, couple_sem, mask_send, mask_recv, halo_send, halo_recv,
    out_send, out_recv, back_send, back_recv, own_sem, store_sem,
):
    me = lax.axis_index("comp")
    tile = lax.axis_index("tile")
    left = lax.rem(tile + tiles - 1, tiles)
    right = lax.rem(tile + 1, tiles)
    comps, columns, rows = block.shape
    freqs = comps // K
    lane_tiles = rows // LANES
    groups = comps // 8
    per = K // 8
    near_first = sorted(range(1, parts), key=lambda d: min(d, parts - d))

    def chunk_load(f):
        part = pl.ds(f * K, K)
        return pltpu.make_async_copy(spectrum.at[part], block.at[part], load_sem.at[f])

    def couple_load():
        return pltpu.make_async_copy(coupling_in, couple, couple_sem)

    smalls = [
        pltpu.make_async_copy(source, target, small_sem.at[i])
        for i, (source, target) in enumerate((
            (table_in, table), (sea_in, sea_own), (depth_in, depth_own),
            (tab_in, tab), (speed_in, wind_speed), (dir_in, wind_dir)))
    ]
    for copy in smalls[:4]:
        copy.start()
    for f in range(freqs):
        chunk_load(f).start()
    for copy in smalls[4:]:
        copy.start()
    couple_load().start()

    barrier = pltpu.get_barrier_semaphore()
    for d in range(1, parts):
        pl.semaphore_signal(barrier, 1, device_id={"comp": lax.rem(me + d, parts)})
    for side in (left, right):
        pl.semaphore_signal(barrier, 1, device_id={"tile": side})

    quarter_of = K // 4
    half = columns // 2
    lane = lax.broadcasted_iota(jnp.int32, (columns, rows), 1)
    sub = lax.broadcasted_iota(jnp.int32, (columns, rows), 0)
    sub_one = lax.broadcasted_iota(jnp.int32, (columns, LANES), 0)

    def find_speed(window, low_sea, high_sea, low_depth, high_depth):
        wet, row = low_sea[...].astype(F32), low_depth[...].astype(F32)
        if window:
            wet = jnp.where(sub < half, wet, high_sea[...].astype(F32))
            row = jnp.where(sub < half, row, high_depth[...].astype(F32))
        sea[window] = wet

        def one(f, carry):
            j = me * freqs + f
            value = jnp.full((columns, rows), table[0, j], F32)
            for d in range(1, DEPTHS):
                value = jnp.where(row == d, table[d, j], value)
            speed[window, f] = value * wet
            return carry

        lax.fori_loop(0, freqs, one, 0)

    def run(alone, beside, f, quarter, low, count, unroll):
        to_east = quarter in (0, 3)
        to_north = quarter in (0, 1)
        halo = west if to_east else east
        first = quarter_of if quarter in (2, 3) else 0
        x_shift = 1 if to_east else columns - 1
        y_shift = 1 if to_north else rows - 1
        inside = (lane > 0) if to_north else (lane < rows - 1)
        windows = ([0] if alone else []) + ([1 if to_east else 2] if beside else [])

        def one(i, carry):
            k = quarter * quarter_of + low + i
            mine = block[f * K + k].astype(F32)
            results = []
            for window in windows:
                energy = mine
                if window:
                    theirs = halo[f, first + low + i].astype(F32)
                    pair = (mine, theirs) if to_east else (theirs, mine)
                    energy = jnp.where(sub < half, *pair)
                cx = speed[window, f] * tab[0, k]
                cy = speed[window, f] * tab[1, k]
                keep = sea[window] - cx - cy
                cy = jnp.where(inside, cy, 0.0)
                for step in range(PSTEPS):
                    energy = keep * energy + cx * pltpu.roll(energy, x_shift, 0) + cy * pltpu.roll(energy, y_shift, 1)
                results.append(energy)
            at = pl.ds(pl.multiple_of(k * 8, 8), 8)
            for p in range(lane_tiles):
                pieces = [energy[:, p * LANES:(p + 1) * LANES] for energy in results]
                if beside:
                    other = pieces[0] if alone else natural[f, p, at, :]
                    pair = (pieces[-1], other) if to_east else (other, pieces[-1])
                    pieces = [jnp.where(sub_one < half, *pair)]
                natural[f, p, at, :] = pieces[0]
            return carry

        lax.fori_loop(0, count, one, 0, unroll=unroll)

    def slot(f, g):
        return f if g == 1 else freqs + 2 * f + g // 2

    def turn(f, pieces):
        def one(p, carry):
            for c, g in pieces:
                value = natural[f, p, pl.ds(64 * g + c, 8, stride=8), :]
                sent[p, c // GCOLS, c % GCOLS, slot(f, g)] = value.astype(BF16)
            return carry

        lax.fori_loop(0, lane_tiles, one, 0)

    early = [(c, 1) for c in range(GCOLS)]
    late = [(c, g) for c in range(GCOLS, columns) for g in range(per)]

    def out_copy(g, low, count, d):
        target = lax.rem(me + d, parts)
        return pltpu.make_async_remote_copy(
            sent.at[target, g, :, pl.ds(low, count)], points.at[g, :, pl.ds(groups * me + low, count)],
            out_send.at[g], out_recv.at[g], device_id={"comp": target})

    for copy in smalls[:4]:
        copy.wait()
    find_speed(0, sea_own, None, depth_own, None)

    def start_alone(f, carry):
        chunk_load(f).wait()
        run(True, False, f, 1, 2, 4, 4)
        run(True, False, f, 2, 0, 4, 4)
        turn(f, early)
        return carry

    start_alone(0, 0)
    pl.semaphore_wait(barrier, parts + 1)

    def mask_copy(side, target, array):
        return pltpu.make_async_remote_copy(
            (sea_in, depth_in)[array],
            (near_sea, near_depth)[array].at[side],
            mask_send.at[side, array], mask_recv.at[side, array],
            device_id={"tile": target},
        )

    def halo_copies(f):
        for part, (first, array, low, target) in enumerate((
                (0, west, 0, right), (1, east, 0, left), (2, east, 1, left), (3, west, 1, right))):
            yield pltpu.make_async_remote_copy(
                spectrum.at[pl.ds(f * K + first * quarter_of, quarter_of)],
                array.at[f, pl.ds(low * quarter_of, quarter_of)],
                halo_send.at[part, f], halo_recv.at[part, f], device_id={"tile": target})

    masks = [mask_copy(side, target, array) for side, target in ((0, right), (1, left)) for array in range(2)]
    for copy in masks:
        copy.start()
    for f in range(freqs):
        for copy in halo_copies(f):
            copy.start()
    for f in range(freqs):
        if f:
            start_alone(f, 0)
        for d in near_first:
            out_copy(0, f, 1, d).start()

    for copy in masks:
        copy.wait()
    find_speed(1, sea_own, near_sea.at[0], depth_own, near_depth.at[0])
    find_speed(2, near_sea.at[1], sea_own, near_depth.at[1], depth_own)

    def finished(f, g):
        turn(f, [(c, g) for c in range(GCOLS)])
        for d in near_first:
            out_copy(0, slot(f, g), 1, d).start()

    def with_halo(f, carry):
        halos = list(halo_copies(f))
        halos[0].wait()
        run(True, True, f, 0, 0, 6, 3)
        halos[1].wait()
        run(True, True, f, 1, 0, 2, 2)
        finished(f, 0)
        run(False, True, f, 1, 2, 4, 4)
        halos[2].wait()
        run(False, True, f, 2, 0, 4, 4)
        run(True, True, f, 2, 4, 2, 2)
        halos[3].wait()
        run(True, True, f, 3, 0, 6, 3)
        finished(f, 2)
        turn(f, late)

        @pl.when(f < AHEAD)
        def _():
            for d in near_first:
                out_copy(1, f, 1, d).start()
            for d in near_first:
                out_copy(1, freqs + 2 * f, 2, d).start()

        return carry

    lax.fori_loop(0, freqs, with_halo, 0)
    for d in near_first:
        out_copy(1, AHEAD, freqs - AHEAD, d).start()
    for d in near_first:
        out_copy(1, freqs + 2 * AHEAD, 2 * (freqs - AHEAD), d).start()

    def own_out(g):
        return pltpu.make_async_copy(
            sent.at[me, g], points.at[g, :, pl.ds(groups * me, groups)], own_sem.at[g])

    for g in range(GROUPS):
        own_out(g).start()

    rows_here = pl.ds(pl.multiple_of(me * LANES, LANES), LANES)
    direction = lax.broadcasted_iota(jnp.int32, (K, LANES), 0).astype(F32) * (2.0 * math.pi / K)
    for copy in smalls[4:]:
        copy.wait()
    for c in range(columns):
        blow = wind_speed[c:c + 1, rows_here]
        heading = wind_dir[c:c + 1, rows_here]
        align = jnp.maximum(jnp.cos(direction - heading), 0.0)
        winds[c // GCOLS, :, (c % GCOLS) * LANES:(c % GCOLS + 1) * LANES] = blow * align
    couple_load().wait()

    total_comps = parts * comps
    two = 2 * K
    width = GCOLS * LANES

    def own_back(g):
        return pltpu.make_async_copy(
            rounded.at[g, pl.ds(pl.multiple_of(comps * me, comps), comps)], back.at[me, g], own_sem.at[2 + g])

    def source(g, carry):
        pltpu.make_async_copy(
            points.at[g, :, pl.ds(0, groups * (parts - 1))],
            points.at[g, :, pl.ds(0, groups * (parts - 1))], out_recv.at[g]).wait()
        own_out(g).wait()

        def weigh(jj, acc, news):
            for h in range(2):
                folded = news[h][0:8] + news[h][8:16] + news[h][16:24]
                acc = acc + tab[2, 2 * jj + h] * folded
            return acc

        def start(z, acc):
            for pair in range(freqs // 2):
                at = pl.ds(pl.multiple_of(comps * z + two * pair, two), two)
                lanes = []
                for c in range(GCOLS):
                    lanes.append(jnp.concatenate([
                        points[g, c, groups * z + slot(2 * pair + h, i)].astype(F32)
                        for h in range(2) for i in range(per)], axis=0))
                whole = jnp.concatenate(lanes, axis=1)
                state[at, :] = whole
                rounded[g, at, :] = whole.astype(BF16)
                acc = weigh(freqs // 2 * z + pair, acc, (whole[:K], whole[K:]))
            return acc

        zero = jnp.zeros((8, width), F32)
        acc = lax.fori_loop(0, parts, start, zero)

        def step(s, acc):
            total = jnp.sum(acc, axis=0, keepdims=True)
            sat = jnp.broadcast_to(total / (total + 100.0), (8, width))
            nonlin[...] = jnp.dot(couple[...], rounded[g], preferred_element_type=F32)

            def update(jj, acc):
                news = []
                for h in range(2):
                    at = pl.ds(pl.multiple_of(two * jj + K * h, K), K)
                    j = 2 * jj + h
                    level = 1.0 - tab[4, j] * sat
                    levels = jnp.concatenate([level] * per, axis=0)
                    rate = levels + tab[3, j] * winds[g]
                    new = jnp.maximum(state[at, :] * rate + 0.125 * nonlin[at, :], 0.0)
                    state[at, :] = new
                    news.append(new)
                rounded[g, pl.ds(pl.multiple_of(two * jj, two), two), :] = jnp.concatenate(news, axis=0).astype(BF16)
                return weigh(jj, acc, news)

            return lax.fori_loop(0, total_comps // two, update, zero)

        lax.fori_loop(0, SRC_STEPS, step, acc)
        for d in near_first:
            target = lax.rem(me + d, parts)
            pltpu.make_async_remote_copy(
                rounded.at[g, pl.ds(pl.multiple_of(comps * target, comps), comps)], back.at[me, g],
                back_send.at[g], back_recv.at[g, g * d], device_id={"comp": target}).start()
        own_back(g).start()
        return carry

    lax.fori_loop(0, GROUPS, source, 0)

    pltpu.make_async_copy(
        back.at[pl.ds(0, parts - 1), 0], back.at[pl.ds(0, parts - 1), 0], back_recv.at[0, 0]).wait()
    own_back(0).wait()

    def place(p, g):
        for c in range(GCOLS):
            value = back[p, g, :, c * LANES:(c + 1) * LANES].astype(F32)
            turned[p, pl.ds(g * GCOLS + c, comps, stride=8), :] = value

    def place_first(p, carry):
        place(p, 0)
        return carry

    lax.fori_loop(0, lane_tiles, place_first, 0)

    def finish(p):
        place(p, 1)
        lanes = pl.ds(pl.multiple_of(p * LANES, LANES), LANES)
        block[:, :, lanes] = turned[p].reshape(comps, columns, LANES).astype(BF16)
        pltpu.make_async_copy(block.at[:, :, lanes], out.at[:, :, lanes], store_sem).start()

    own_back(1).wait()
    finish(me)

    def arrived(i, carry):
        d = (i % 2) * (parts - 1 - i // 2) + (1 - i % 2) * (1 + i // 2)
        pltpu.make_async_copy(back.at[0, 1], back.at[0, 1], back_recv.at[1, d]).wait()
        finish(lax.rem(me + parts - d, parts))
        return carry

    lax.fori_loop(0, parts - 1, arrived, 0)
    pltpu.make_async_copy(block, out, store_sem).wait()

    for g in range(GROUPS):
        pltpu.make_async_copy(
            sent.at[pl.ds(0, parts - 1), g], sent.at[pl.ds(0, parts - 1), g], out_send.at[g]).wait()
        span = pl.ds(0, comps * (parts - 1))
        pltpu.make_async_copy(rounded.at[g, span], rounded.at[g, span], back_send.at[g]).wait()


def on_device(parts, tiles, spectrum, sea_mask, depth_class, group_speed, wind_speed, wind_dir, coupling):
    comps, columns, rows = spectrum.shape
    freqs = comps // K
    whole = comps * parts
    width = GCOLS * LANES
    tab = jnp.asarray(tables())
    hbm = pl.BlockSpec(memory_space=pltpu.HBM)
    dma = pltpu.SemaphoreType.DMA
    return pl.pallas_call(
        functools.partial(step_kernel, parts, tiles),
        out_shape=jax.ShapeDtypeStruct(spectrum.shape, BF16),
        in_specs=[hbm] * 8,
        out_specs=hbm,
        scratch_shapes=[
            pltpu.SMEM(tab.shape, F32),
            pltpu.SMEM(group_speed.shape, F32),
            pltpu.VMEM((columns, rows), jnp.int32),
            pltpu.VMEM((columns, rows), jnp.int32),
            pltpu.VMEM((columns, rows), F32),
            pltpu.VMEM((columns, rows), F32),
            pltpu.VMEM((comps, columns, rows), BF16),
            pltpu.VMEM((freqs, K // 2, columns, rows), BF16),
            pltpu.VMEM((freqs, K // 2, columns, rows), BF16),
            pltpu.VMEM((2, columns, rows), jnp.int32),
            pltpu.VMEM((2, columns, rows), jnp.int32),
            pltpu.VMEM((3, freqs, columns, rows), F32),
            pltpu.VMEM((3, columns, rows), F32),
            pltpu.VMEM((freqs, parts, K * 8, LANES), F32),
            pltpu.VMEM((parts, GROUPS, GCOLS, comps // 8, 8, LANES), BF16),
            pltpu.VMEM((GROUPS, GCOLS, whole // 8, 8, LANES), BF16),
            pltpu.VMEM((whole, whole), BF16),
            pltpu.VMEM((whole, width), F32),
            pltpu.VMEM((whole, width), F32),
            pltpu.VMEM((GROUPS, whole, width), BF16),
            pltpu.VMEM((GROUPS, K, width), F32),
            pltpu.VMEM((parts, GROUPS, comps, width), BF16),
            pltpu.VMEM((parts, comps * 8, LANES), F32),
            dma((6,)), dma((freqs,)), dma,
            dma((2, 2)), dma((2, 2)), dma((4, freqs)), dma((4, freqs)),
            dma((GROUPS,)), dma((GROUPS,)), dma((GROUPS,)), dma((GROUPS, parts)), dma((2 * GROUPS,)), dma,
        ],
        compiler_params=pltpu.CompilerParams(collective_id=0, has_side_effects=True, vmem_limit_bytes=48 << 20),
    )(*(pltpu.with_memory_space_constraint(a, pltpu.HBM) for a in (tab, group_speed, sea_mask, depth_class, wind_speed, wind_dir, spectrum, coupling)))


def solution(mesh):
    placed = (
        P("comp", "tile", None),
        P("tile", None),
        P("tile", None),
        P(),
        P("tile", None),
        P("tile", None),
        P(),
    )
    return jax.shard_map(
        functools.partial(on_device, mesh.shape["comp"], mesh.shape["tile"]),
        mesh=mesh, in_specs=placed, out_specs=P("comp", "tile", None), check_vma=False,
    )
```
